768 devices in a mesh: prow: 64 (over y, x, core), pcol: 12 (over z).
Axes of the slice: x: 4, y: 8, z: 12, core: 2. Of those that a mesh axis runs over, the one named last changes fastest.
Arguments:
- matrix: float32 [49152, 9216], P('prow', 'pcol'), may hold values from -6 to 6
- panel: float32 [49152, 512], P(('prow', 'pcol')), may hold values from -0.25 to 0.3
- pivot_rows: int32 [512], replicated, may hold values from 0 to 49151, as said below
Outputs:
- factored: float32 [49152, 9216], P('prow', 'pcol')
The draws below stay inside these ranges and needn't reach their ends.
Inputs may be any that keep to these rules, and one draw needn't show every extreme that they name: `pivot_rows`: the entries are distinct; 0 and 49151 always occur.
All inputs are finite; a program needn't handle non-finite values.
Results may differ from the reference program's by a relative error of at most 0.00005.
Values sent between devices are 32-bit elements; how exact they have to be, the bound alone decides.
A program may use at most 32 MiB of HBM per device.

```python
import math
import jax
import jax.numpy as jnp
from jax import lax

NB = 512
ROWS = 49152
COLS = 9216


def draw_pivot_rows(key, part):
    picked = jax.random.permutation(key, ROWS)[:NB].astype(jnp.int32)
    picked = picked.at[jnp.argmax(picked)].set(ROWS - 1)
    picked = picked.at[jnp.argmin(picked)].set(0)
    return picked


def draw_panel(key, part):
    lead_key = jax.random.fold_in(key, 101)
    rest_key = jax.random.fold_in(key, 202)
    lead = jax.random.uniform(lead_key, (NB, NB), jnp.float32, 0.15, 0.25)
    spread = 1.0 / math.sqrt(NB)
    rest = jax.random.normal(rest_key, (ROWS - NB, NB), jnp.float32) * spread
    rest = jnp.clip(rest, -0.25, 0.25)
    return jnp.concatenate([lead, rest], axis=0)


def block_scale(own_key, extent, shards, low, top_value):
    def one(axis_at, parts):
        steps = jax.random.uniform(jax.random.fold_in(jax.random.fold_in(own_key, 6), axis_at), (parts,), jnp.float32, low / len(shards), top_value / len(shards))
        return jnp.repeat(jnp.exp(steps), extent[axis_at] // parts).reshape((-1,) + (1,) * (len(extent) - axis_at - 1))

    gain = one(*shards[0])
    for cut in shards[1:]:
        gain = gain * one(*cut)
    return gain


def gaussian(own_key, shape, width, limit, split=(), held_as=jnp.bfloat16):
    result = width * jax.random.normal(own_key, shape, jnp.float32)
    if split:
        result = result * block_scale(own_key, shape, split, -0.22, 0.18)
    return jnp.clip(result, -limit, limit).astype(held_as)


def setup_inputs(seed: int = 0) -> dict:
    arg_keys = jax.random.split(jax.random.key(seed), 4)
    return {
        "matrix": gaussian(arg_keys[0], (ROWS, COLS), 1.0, 6.0, ((0, 64), (1, 12)), jnp.float32),
        "panel": draw_panel(jax.random.fold_in(arg_keys[3], 71), 0),
        "pivot_rows": draw_pivot_rows(jax.random.fold_in(arg_keys[3], 71), 0),
    }


def reference(matrix, panel, pivot_rows):
    total_rows = matrix.shape[0]
    new_top = jnp.take(matrix, pivot_rows, axis=0)
    vacated = pivot_rows >= NB
    vac_sorted = jnp.sort(jnp.where(vacated, pivot_rows, total_rows))
    top_index = jnp.arange(NB, dtype=jnp.int32)
    chosen = jnp.any(pivot_rows[None, :] == top_index[:, None], axis=1)
    left_sorted = jnp.sort(jnp.where(chosen, NB, top_index))
    source_rows = jnp.take(matrix, jnp.minimum(left_sorted, NB - 1), axis=0)
    swapped = matrix.at[vac_sorted].set(source_rows, mode='drop')
    lower_block = panel[:NB]
    upper_block = lax.linalg.triangular_solve(lower_block, new_top, left_side=True, lower=True, unit_diagonal=True)
    updated = swapped[NB:] - jnp.dot(panel[NB:].astype(jnp.float32), upper_block.astype(jnp.float32), precision=lax.Precision.HIGHEST, preferred_element_type=jnp.float32)
    return jnp.concatenate([upper_block, updated], axis=0)
```

```python
import functools

import jax
import jax.numpy as jnp
from jax import lax
from jax.experimental import pallas as pl
from jax.experimental.pallas import tpu as pltpu
from jax.sharding import PartitionSpec as P

NB = 512
NX, NY, NZ = 4, 8, 12
CHIPS = NX * NY
CAP = 32
MESH = pl.DeviceIdType.MESH
F32, BF16, I32 = jnp.float32, jnp.bfloat16, jnp.int32
HIGHEST = lax.Precision.HIGHEST


def mm(a, b, dims=((1,), (0,))):
    return lax.dot_general(a, b, (dims, ((), ())), preferred_element_type=F32)


def split3(v):
    hi = v.astype(BF16)
    rest = v - hi.astype(F32)
    mid = rest.astype(BF16)
    low = (rest - mid.astype(F32)).astype(BF16)
    return hi, mid, low


def select_rows(onehot, v, dims=((1,), (0,))):
    hi, mid, low = split3(v)
    return (mm(onehot, low, dims) + mm(onehot, mid, dims)) + mm(onehot, hi, dims)


def iota(shape, axis):
    return lax.broadcasted_iota(I32, shape, axis)


def chip_of(rows):
    return ((rows >> 9) * 171) >> 9


def count(mask, axis):
    return jnp.sum(mask.astype(F32), axis=axis, keepdims=True).astype(I32)


def prep_kernel(me_ref, prow_ref, pcol_ref, m_ref,
                contrib_ref, sel_ref, dest_ref, ok_ref, top_ref):
    me = me_ref[0]
    rows = m_ref.shape[0]
    half = m_ref.shape[1] // 2
    p_r = prow_ref[...]
    p_c = jnp.broadcast_to(pcol_ref[...], (NB, NB))
    c_r, c_c = chip_of(p_r), chip_of(p_c)
    i0, i1 = iota((NB, NB), 0), iota((NB, NB), 1)
    same = c_c == c_r
    slot_r = count(same & (i0 < i1), 0)
    slot_c = count(same & (i1 < i0), 1)
    d_r = c_r * CAP + slot_r
    dest_ref[...] = jnp.broadcast_to(c_c[:, :1] * CAP + slot_c, dest_ref.shape)
    ok_ref[...] = jnp.broadcast_to(jnp.max(slot_r, axis=1, keepdims=True), ok_ref.shape)
    mine = d_r == (me >> 1) * CAP + iota((CAP, NB), 0)
    row = jnp.sum(jnp.where(mine, (p_r + 1).astype(F32), 0.0), axis=1, keepdims=True).astype(I32) - 1
    pick = (row - me * rows) == iota((CAP, rows), 1)
    got = select_rows(pick.astype(BF16), m_ref[...])
    contrib_ref[0] = got[:, :half]
    contrib_ref[1] = got[:, half:]
    sel_ref[...] = (pick & (row >= NB)).astype(F32)

    @pl.when(me == 0)
    def _():
        t_r = iota((1, NB), 1)
        left_rank = t_r - count(p_c < t_r, 0)
        chosen = count(p_c == t_r, 0) > 0
        left_key = jnp.where(chosen, -2, left_rank)
        vac_rank = count((p_c >= NB) & (p_c < p_r), 0)
        vac_key = jnp.where(p_r >= NB, vac_rank + 1, 0).astype(F32)
        parts = split3(m_ref[:NB])

        @pl.loop(0, CHIPS // 8)
        def _(g):
            rows_at = 8 * CAP
            e = d_r == g * rows_at + iota((rows_at, NB), 0)
            key = jnp.sum(jnp.where(e, vac_key, 0.0), axis=1, keepdims=True).astype(I32) - 1
            onehot = (key == left_key).astype(BF16)
            out = (mm(onehot, parts[2]) + mm(onehot, parts[1])) + mm(onehot, parts[0])
            top_ref[pl.ds(g * 8, 8), 0] = out[:, :half].reshape(8, CAP, half)
            top_ref[pl.ds(g * 8, 8), 1] = out[:, half:].reshape(8, CAP, half)


def prep(me, p_row, p_col, matrix):
    half = matrix.shape[1] // 2
    vm = pl.BlockSpec(memory_space=pltpu.VMEM)
    return pl.pallas_call(
        prep_kernel,
        out_shape=(
            jax.ShapeDtypeStruct((2, CAP, half), F32),
            jax.ShapeDtypeStruct((CAP, matrix.shape[0]), F32),
            jax.ShapeDtypeStruct((NB, 128), I32),
            jax.ShapeDtypeStruct((8, 128), I32),
            jax.ShapeDtypeStruct((CHIPS, 2, CAP, half), F32),
        ),
        in_specs=[pl.BlockSpec(memory_space=pltpu.SMEM), vm, vm, vm],
        out_specs=(vm,) * 5,
        name="prep",
    )(me, p_row, p_col, matrix)


class Ring:
    def __init__(self, n, me, piece, device, send, recv):
        self.n, self.me, self.piece, self.device = n, me, piece, device
        self.send, self.recv = send, recv
        self.waited = set()

    def moves(self, s):
        last = s == self.n // 2 - 1
        return [(d, h) for h in (0, 1) for d in (0, 1) if not (last and d != h)]

    def copy(self, s, d, h, block):
        n = self.n
        ref = self.piece(lax.rem(block + 2 * n, n), h)
        peer = lax.rem(self.me + (1 if d == 0 else n - 1), n)
        return pltpu.make_async_remote_copy(
            src_ref=ref, dst_ref=ref,
            send_sem=self.send.at[d, s, h], recv_sem=self.recv.at[d, s, h],
            device_id=self.device(peer), device_id_type=MESH)

    def out(self, s, d, h):
        return self.copy(s, d, h, self.me - s if d == 0 else self.me + s)

    def arrive(self, s, d, h):
        block = self.me - 1 - s if d == 0 else self.me + 1 + s
        self.copy(s, d, h, block).wait_recv()
        self.waited.add((s, d, h))
        return lax.rem(block + 2 * self.n, self.n)

    def step(self, s, hook=None):
        for d, h in self.moves(s):
            if s > 0:
                block = self.arrive(s - 1, d, h)
                if hook is not None:
                    hook(block, h)
            self.out(s, d, h).start()

    def finish(self, hook=None):
        for s in range(self.n // 2):
            for d, h in self.moves(s):
                if (s, d, h) not in self.waited:
                    block = self.arrive(s, d, h)
                    if hook is not None:
                        hook(block, h)

    def drain(self):
        for s in range(self.n // 2):
            for d, h in self.moves(s):
                self.out(s, d, h).wait_send()


def exchange_kernel(panel_ref, contrib_ref, top_ref,
                    pall_ref, slots_ref, low_ref, tops_ref,
                    from_pair, own, low_in,
                    z_send, z_recv, r_send, r_recv, q_send, q_recv,
                    one_send, one_recv, lone_send, lone_recv,
                    zl_send, zl_recv, sc_send, sc_recv, local,
                    pair_send, pair_recv, slot_send, slot_recv,
                    lpair_send, lpair_recv, top_send, top_recv, tp_send, tp_recv):
    pr = lax.axis_index("prow")
    z = lax.axis_index("pcol")
    core = lax.rem(pr, 2)
    chip = pr // 2
    x = lax.rem(chip, NX)
    y = chip // NX
    half = own.shape[1]

    def dev(x=x, y=y, c=core, z=z):
        return ((y * NX + x) * 2 + c, z)

    def remote(src, dst, ss, rs, device):
        return pltpu.make_async_remote_copy(
            src_ref=src, dst_ref=dst, send_sem=ss, recv_sem=rs,
            device_id=device, device_id_type=MESH)

    partner = dev(c=1 - core)
    is_root = pr == 0
    barrier = pltpu.get_barrier_semaphore()

    def hello(device):
        pl.semaphore_signal(barrier, inc=1, device_id=device, device_id_type=MESH)

    for d in range(1, NZ):
        hello(dev(z=lax.rem(z + d, NZ)))
    for d in range(1, NX):
        hello(dev(x=lax.rem(x + d, NX)))
    for d in range(1, NY):
        hello(dev(y=lax.rem(y + d, NY)))
    hello(partner)
    near = NZ + NX + NY - 2

    @pl.when(is_root)
    def _():
        @pl.loop(1, 2 * CHIPS)
        def _(q):
            hello((q, z))
        pl.semaphore_wait(barrier, near + 2 * CHIPS - 1)

    @pl.when(jnp.logical_not(is_root))
    def _():
        hello((0, z))
        pl.semaphore_wait(barrier, near + 1)

    pltpu.make_async_copy(panel_ref, pall_ref.at[z], local.at[0]).start()
    pltpu.make_async_copy(panel_ref, pall_ref.at[z], local.at[0]).wait()

    def line(mine):
        other = 1 - mine
        n1, n2 = (NX, NY) if mine == 0 else (NY, NX)
        a1, a2 = (x, y) if mine == 0 else (y, x)
        peer1 = (lambda i: dev(x=i)) if mine == 0 else (lambda i: dev(y=i))
        peer2 = (lambda i: dev(y=i)) if mine == 0 else (lambda i: dev(x=i))
        slots = slots_ref.at[mine]
        lows = low_ref.at[mine]

        def part(ref):
            if mine == 0:
                return lambda b, h: ref.at[b, pl.ds(2 * h, 2)]
            return lambda b, h: ref.at[pl.ds(4 * h, 4), b]

        def whole(ref, b):
            return ref.at[b] if mine == 0 else ref.at[:, b]

        zr = Ring(NZ, z, lambda b, h: pall_ref.at[b, pl.ds(32 * h, 32)],
                  lambda i: dev(z=i), z_send, z_recv)
        has_low = (z < NB // 64) & (lax.rem(z, 2) == mine)
        zr.step(0)

        @pl.when(is_root & (z < NB // 64))
        def _():
            @pl.loop(0, CHIPS)
            def _(q):
                src = panel_ref.at[pl.ds(pl.multiple_of(q // NX * 8, 8), 8),
                                   pl.ds(pl.multiple_of(lax.rem(q, NX) * 128, 128), 128)]

                @pl.when((q > 0) | (lax.rem(z, 2) == 1))
                def _():
                    remote(src, low_in, sc_send.at[q], sc_recv,
                           (q * 2 + lax.rem(z, 2), z)).start()

        @pl.when(is_root & has_low)
        def _():
            pltpu.make_async_copy(panel_ref.at[pl.ds(0, 8), pl.ds(0, 128)], low_in, local.at[1]).start()
            pltpu.make_async_copy(panel_ref.at[pl.ds(0, 8), pl.ds(0, 128)], low_in, local.at[1]).wait()

        pair = remote(contrib_ref.at[other], from_pair, pair_send, pair_recv, partner)
        pair.start()

        @pl.when(is_root)
        def _():
            remote(top_ref.at[0, 1], tops_ref.at[1], tp_send.at[1], top_recv, partner).start()

            @pl.loop(1, CHIPS)
            def _(q):
                for c in (0, 1):
                    remote(top_ref.at[q, c], tops_ref.at[c], top_send, top_recv, (q * 2 + c, z)).start()

        pair.wait_recv()
        own[...] = contrib_ref[mine] + from_pair[...]
        keep = pltpu.make_async_copy(own, slots.at[y, x], local.at[2])
        keep.start()
        first = []
        for d in range(1, n1):
            first.append(remote(own, slots.at[y, x], one_send.at[d], one_recv.at[d],
                                peer1(lax.rem(a1 + d, n1))))
            first[-1].start()
        zr.step(1)

        @pl.when(has_low)
        def _():
            @pl.when(jnp.logical_not(is_root & (mine == 0)))
            def _():
                remote(low_in, low_in, sc_send.at[0], sc_recv, partner).wait_recv()
            pltpu.make_async_copy(low_in, lows.at[y, x, z // 2], local.at[3]).start()
            for d in range(1, NZ):
                remote(low_in, lows.at[y, x, z // 2], zl_send.at[d], zl_recv.at[z // 2],
                       dev(z=lax.rem(z + d, NZ))).start()

        zr.step(2)
        keep.wait()
        for d in range(1, n1):
            src = lax.rem(a1 + n1 - d, n1)
            dst = slots.at[y, src] if mine == 0 else slots.at[src, x]
            remote(dst, dst, one_send.at[d], one_recv.at[d], peer1(src)).wait_recv()
        ring = Ring(n2, a2, part(slots), peer2, r_send, r_recv)
        ring.step(0)

        def to_pair(block, h):
            remote(part(slots)(block, h), part(slots)(block, h), slot_send, slot_recv, partner).start()

        def first_pair():
            for h in (0, 1):
                to_pair(a2, h)

        first_pair()
        zr.step(3)
        for i in range(4):
            @pl.when(z != 2 * i + mine)
            def _():
                ref = lows.at[y, x, i]
                remote(ref, ref, zl_send.at[1], zl_recv.at[i], partner).wait_recv()

        @pl.when(has_low)
        def _():
            pltpu.make_async_copy(low_in, lows.at[y, x, z // 2], local.at[3]).wait()
        lfirst = []
        for d in range(1, n1):
            lfirst.append(remote(lows.at[y, x], lows.at[y, x], lone_send.at[d], lone_recv.at[d],
                                 peer1(lax.rem(a1 + d, n1))))
            lfirst[-1].start()
        ring.step(1, to_pair)
        zr.step(4)
        for d in range(1, n1):
            src = lax.rem(a1 + n1 - d, n1)
            dst = lows.at[y, src] if mine == 0 else lows.at[src, x]
            remote(dst, dst, lone_send.at[d], lone_recv.at[d], peer1(src)).wait_recv()
        lring = Ring(n2, a2, part(lows), peer2, q_send, q_recv)
        lring.step(0)
        for s in range(2, n2 // 2):
            ring.step(s, to_pair)
            if s == 2:
                zr.step(5)
            lring.step(s - 1)
        if n2 // 2 <= 2:
            zr.step(5)
        lring.step(n2 // 2 - 1)
        ring.finish(to_pair)
        lring.finish()
        lpair = remote(lows, lows, lpair_send, lpair_recv, partner)
        lpair.start()

        @pl.when(jnp.logical_not(is_root & (mine == 0)))
        def _():
            remote(tops_ref.at[mine], tops_ref.at[mine], top_send, top_recv, partner).wait_recv()

        @pl.when(is_root & (mine == 0))
        def _():
            pltpu.make_async_copy(top_ref.at[0, 0], tops_ref.at[0], local.at[4]).start()
            pltpu.make_async_copy(top_ref.at[0, 0], tops_ref.at[0], local.at[4]).wait()
        tpair = remote(tops_ref.at[mine], tops_ref.at[mine], tp_send.at[0], tp_recv, partner)
        tpair.start()

        zr.finish()
        remote(slots_ref.at[other], slots_ref.at[other], slot_send, slot_recv, partner).wait_recv()
        remote(low_ref.at[other], low_ref.at[other], lpair_send, lpair_recv, partner).wait_recv()
        remote(tops_ref.at[other], tops_ref.at[other], tp_send.at[0], tp_recv, partner).wait_recv()

        pair.wait_send()
        for c in first + lfirst + [lpair, tpair]:
            c.wait_send()
        ring.drain()
        lring.drain()
        zr.drain()
        remote(slots, slots, slot_send, slot_recv, partner).wait_send()

        @pl.when(has_low)
        def _():
            for d in range(1, NZ):
                remote(low_in, lows.at[y, x, z // 2], zl_send.at[d], zl_recv.at[z // 2],
                       dev(z=lax.rem(z + d, NZ))).wait_send()

        @pl.when(is_root & (z < NB // 64))
        def _():
            @pl.loop(0, CHIPS)
            def _(q):
                @pl.when((q > 0) | (lax.rem(z, 2) == 1))
                def _():
                    remote(low_in, low_in, sc_send.at[q], sc_recv, partner).wait_send()

        @pl.when(is_root)
        def _():
            remote(top_ref.at[0, 1], tops_ref.at[1], tp_send.at[1], top_recv, partner).wait_send()
            rest = top_ref.at[pl.ds(1, CHIPS - 1)]
            remote(rest, rest, top_send, top_recv, partner).wait_send()

    for mine in (0, 1):
        @pl.when(core == mine)
        def _(mine=mine):
            line(mine)


def exchange(panel, contrib, tops):
    half = contrib.shape[2]
    dma = pltpu.SemaphoreType.DMA
    anyspec = pl.BlockSpec(memory_space=pl.ANY)
    vm = pl.BlockSpec(memory_space=pltpu.VMEM)
    return pl.pallas_call(
        exchange_kernel,
        out_shape=(
            jax.ShapeDtypeStruct((NZ,) + panel.shape, F32),
            jax.ShapeDtypeStruct((2, NY, NX, CAP, half), F32),
            jax.ShapeDtypeStruct((2, NY, NX, 4, 8, 128), F32),
            jax.ShapeDtypeStruct((2, CAP, half), F32),
        ),
        in_specs=[vm, vm, anyspec],
        out_specs=(anyspec,) * 4,
        scratch_shapes=[
            pltpu.VMEM((CAP, half), F32),
            pltpu.VMEM((CAP, half), F32),
            pltpu.VMEM((8, 128), F32),
            dma((2, NZ // 2, 2)), dma((2, NZ // 2, 2)),
            dma((2, NY // 2, 2)), dma((2, NY // 2, 2)),
            dma((2, NY // 2, 2)), dma((2, NY // 2, 2)),
            dma((NY,)), dma((NY,)), dma((NY,)), dma((NY,)),
            dma((NZ,)), dma((4,)), dma((CHIPS,)), dma, dma((5,)),
            dma, dma, dma, dma, dma, dma, dma, dma, dma((2,)), dma,
        ],
        compiler_params=pltpu.CompilerParams(collective_id=0, has_side_effects=True),
        name="exchange",
    )(panel, contrib, tops)


def finish_kernel(me_ref, m_ref, pall_ref, slots_ref, low_ref, tops_ref, sel_ref, dest_ref,
                  out_ref, lower, inverse, p_hi, p_lo, perm):
    me = me_ref[0]
    rows = m_ref.shape[0]

    @pl.when(pl.program_id(0) == 0)
    def _():
        for i in range(NB // 64):
            for yy in range(NY):
                for xx in range(NX):
                    if 128 * xx < 64 * i + 64:
                        lower[64 * i + 8 * yy:64 * i + 8 * yy + 8, 128 * xx:128 * xx + 128] = (
                            low_ref[i % 2, yy, xx, i // 2])
        i0, i1 = iota((128, 128), 0), iota((128, 128), 1)
        eye = (i0 == i1).astype(F32)
        diag = [lower[128 * k:128 * k + 128, 128 * k:128 * k + 128] for k in range(4)]
        size = 1
        invs = [eye] * 4
        while size < 128:
            mask = ((i0 // (2 * size)) == (i1 // (2 * size))) & (
                (i0 // size) % 2 == 1) & ((i1 // size) % 2 == 0)
            offs = [jnp.where(mask, d, 0.0) for d in diag]
            if size == 1:
                invs = [eye - o for o in offs]
            else:
                mids = [jnp.dot(o, v, precision=HIGHEST, preferred_element_type=F32)
                        for o, v in zip(offs, invs)]
                invs = [v - jnp.dot(v, t, precision=HIGHEST, preferred_element_type=F32)
                        for v, t in zip(invs, mids)]
            size *= 2
        for k in range(4):
            inverse[k] = invs[k]
        full = pall_ref[...]
        hi = full.astype(BF16)
        p_hi[...] = hi
        p_lo[...] = (full - hi.astype(F32)).astype(BF16)
        for k in range(CHIPS * CAP // 128):
            perm[:, 128 * k:128 * k + 128] = (
                dest_ref[...] == iota((NB, 128), 1) + 128 * k).astype(BF16)

    top = select_rows(perm[...], slots_ref[0])
    done = []
    for i in range(4):
        rhs = top[128 * i:128 * i + 128]
        if i:
            rhs = rhs - jnp.dot(lower[128 * i:128 * i + 128, :128 * i],
                                jnp.concatenate(done, axis=0) if i > 1 else done[0],
                                precision=HIGHEST, preferred_element_type=F32)
        done.append(jnp.dot(inverse[i], rhs, precision=HIGHEST, preferred_element_type=F32))
    upper = jnp.concatenate(done, axis=0)
    u_hi = upper.astype(BF16)
    u_lo = (upper - u_hi.astype(F32)).astype(BF16)
    product = (mm(p_lo[...], u_hi) + mm(p_hi[...], u_lo)) + mm(p_hi[...], u_hi)
    sel = sel_ref[...].astype(BF16)
    incoming = select_rows(sel, tops_ref[0], ((0,), (0,)))
    replaced = mm(sel, jnp.ones((CAP, 128), BF16), ((0,), (0,)))[:, :1] > 0.5
    out_ref[...] = jnp.where(replaced, incoming, m_ref[...]) - product

    @pl.when(me == 0)
    def _():
        out_ref[:NB] = upper


def finish(me, matrix, pall, slots, low, tops, sel, dest):
    rows, cols = matrix.shape
    half = cols // 2
    whole = lambda shape: pl.BlockSpec(shape, lambda n: (0,) * len(shape))
    return pl.pallas_call(
        finish_kernel,
        grid=(2,),
        out_shape=jax.ShapeDtypeStruct(matrix.shape, F32),
        in_specs=[
            pl.BlockSpec(memory_space=pltpu.SMEM),
            pl.BlockSpec((rows, half), lambda n: (0, n)),
            whole((rows, NB)),
            pl.BlockSpec((1, CHIPS * CAP, half), lambda n: (n, 0, 0)),
            whole(low.shape),
            pl.BlockSpec((1, CAP, half), lambda n: (n, 0, 0)),
            whole(sel.shape),
            whole(dest.shape),
        ],
        out_specs=pl.BlockSpec((rows, half), lambda n: (0, n)),
        scratch_shapes=[
            pltpu.VMEM((NB, NB), F32),
            pltpu.VMEM((4, 128, 128), F32),
            pltpu.VMEM((rows, NB), BF16),
            pltpu.VMEM((rows, NB), BF16),
            pltpu.VMEM((NB, CHIPS * CAP), BF16),
        ],
        name="finish",
    )(me, matrix, pall.reshape(rows, NB), slots.reshape(2, CHIPS * CAP, half), low, tops, sel, dest)


def ring_sum(value, axis):
    n = lax.axis_size(axis)
    pairs = [(i, (i + 1) % n) for i in range(n)]

    def body(_, carry):
        total, moving = carry
        moving = lax.ppermute(moving, axis, pairs)
        return total + moving, moving

    return lax.fori_loop(0, n - 1, body, (value, value))[0]


def dense(matrix, panel, pivot_rows):
    own_rows = matrix.shape[0]
    row = lax.axis_index("prow")
    col = lax.axis_index("pcol")
    row_base = row * own_rows
    slab = jnp.zeros((lax.axis_size("pcol"),) + panel.shape, F32)
    panels = ring_sum(lax.dynamic_update_slice(slab, panel[None], (col, 0, 0)), "pcol")
    panels = panels.reshape(own_rows, NB)
    local_rows = pivot_rows - row_base
    owned = (local_rows >= 0) & (local_rows < own_rows)
    picked = (local_rows[:, None] == jnp.arange(own_rows, dtype=I32)[None, :]).astype(F32)
    picked = jnp.dot(picked, matrix, precision=HIGHEST, preferred_element_type=F32)
    first = jnp.where(row == 0, 1.0, 0.0)
    pack = jnp.concatenate([picked, matrix[:NB] * first], axis=1)
    pack = jnp.concatenate([pack, panels[:NB] * first], axis=1)
    pack = ring_sum(pack, "prow")
    own_cols = matrix.shape[1]
    new_top, top_rows, lower = pack[:, :own_cols], pack[:, own_cols:2 * own_cols], pack[:, 2 * own_cols:]

    def solve_row(j, upper):
        coef = lax.dynamic_slice(lower, (j, 0), (1, NB))
        coef = jnp.where(jnp.arange(NB)[None, :] < j, coef, 0.0)
        done = jnp.dot(coef, upper, precision=HIGHEST, preferred_element_type=F32)
        mine = lax.dynamic_slice(upper, (j, 0), (1, own_cols)) - done
        return lax.dynamic_update_slice(upper, mine, (j, 0))

    upper = lax.fori_loop(0, NB, solve_row, new_top)
    vacated = pivot_rows >= NB
    top_index = jnp.arange(NB, dtype=I32)
    chosen = jnp.any(pivot_rows[None, :] == top_index[:, None], axis=1)
    left_rank = top_index - jnp.sum((pivot_rows[None, :] < top_index[:, None]).astype(I32), axis=1)
    vac_rank = jnp.sum((vacated[None, :] & (pivot_rows[None, :] < pivot_rows[:, None])).astype(I32), axis=1)
    pairing = (vacated[:, None] & jnp.logical_not(chosen)[None, :]
               & (left_rank[None, :] == vac_rank[:, None])).astype(F32)
    incoming = jnp.dot(pairing, top_rows, precision=HIGHEST, preferred_element_type=F32)
    global_rows = row_base + jnp.arange(own_rows, dtype=I32)
    place = (global_rows[:, None] == pivot_rows[None, :]) & vacated[None, :]
    moved = jnp.dot(place.astype(F32), incoming, precision=HIGHEST, preferred_element_type=F32)
    swapped = jnp.where(jnp.any(place, axis=1)[:, None], moved, matrix)
    updated = swapped - jnp.dot(panels, upper, precision=HIGHEST, preferred_element_type=F32)
    top_fill = jnp.pad(upper, ((0, own_rows - NB), (0, 0)))
    return jnp.where((global_rows < NB)[:, None], top_fill, updated)


def shards(matrix, panel, pivot_rows):
    me = lax.axis_index("prow").reshape(1)
    contrib, sel, dest, most, tops = prep(me, pivot_rows.reshape(1, NB), pivot_rows.reshape(NB, 1), matrix)

    def fast(_):
        pall, slots, low, top = exchange(panel, contrib, tops)
        return finish(me, matrix, pall, slots, low, top, sel, dest)

    def slow(_):
        return dense(matrix, panel, pivot_rows)

    return lax.cond(most[0, 0] < CAP, fast, slow, 0)


def solution(mesh):
    return jax.shard_map(
        shards,
        mesh=mesh,
        in_specs=(P("prow", "pcol"), P(("prow", "pcol"), None), P()),
        out_specs=P("prow", "pcol"),
        check_vma=False,
    )
```

```python
import functools

import jax
import jax.numpy as jnp
from jax import lax
from jax.experimental import pallas as pl
from jax.experimental.pallas import tpu as pltpu
from jax.sharding import PartitionSpec as P

NB = 512
NX, NY, NZ = 4, 8, 12
CHIPS = NX * NY
CAP = 32
MESH = pl.DeviceIdType.MESH
F32, BF16, I32 = jnp.float32, jnp.bfloat16, jnp.int32
HIGHEST = lax.Precision.HIGHEST


def mm(a, b, dims=((1,), (0,))):
    return lax.dot_general(a, b, (dims, ((), ())), preferred_element_type=F32)


def split3(v):
    hi = v.astype(BF16)
    rest = v - hi.astype(F32)
    mid = rest.astype(BF16)
    low = (rest - mid.astype(F32)).astype(BF16)
    return hi, mid, low


def select_rows(onehot, v, dims=((1,), (0,))):
    hi, mid, low = split3(v)
    return (mm(onehot, low, dims) + mm(onehot, mid, dims)) + mm(onehot, hi, dims)


def iota(shape, axis):
    return lax.broadcasted_iota(I32, shape, axis)


def chip_of(rows):
    return ((rows >> 9) * 171) >> 9


def count(mask, axis):
    return jnp.sum(mask.astype(F32), axis=axis, keepdims=True).astype(I32)


class Ring:
    def __init__(self, n, me, piece, device, send, recv):
        self.n, self.me, self.piece, self.device = n, me, piece, device
        self.send, self.recv = send, recv
        self.waited = set()

    def moves(self, s):
        last = s == self.n // 2 - 1
        return [(d, h) for h in (0, 1) for d in (0, 1) if not (last and d != h)]

    def copy(self, s, d, h, block):
        n = self.n
        ref = self.piece(lax.rem(block + 2 * n, n), h)
        peer = lax.rem(self.me + (1 if d == 0 else n - 1), n)
        return pltpu.make_async_remote_copy(
            src_ref=ref, dst_ref=ref,
            send_sem=self.send.at[d, s, h], recv_sem=self.recv.at[d, s, h],
            device_id=self.device(peer), device_id_type=MESH)

    def out(self, s, d, h):
        return self.copy(s, d, h, self.me - s if d == 0 else self.me + s)

    def arrive(self, s, d, h):
        block = self.me - 1 - s if d == 0 else self.me + 1 + s
        self.copy(s, d, h, block).wait_recv()
        self.waited.add((s, d, h))
        return lax.rem(block + 2 * self.n, self.n)

    def step(self, s, hook=None):
        for d, h in self.moves(s):
            if s > 0:
                block = self.arrive(s - 1, d, h)
                if hook is not None:
                    hook(block, h)
            self.out(s, d, h).start()

    def finish(self, hook=None):
        for s in range(self.n // 2):
            for d, h in self.moves(s):
                if (s, d, h) not in self.waited:
                    block = self.arrive(s, d, h)
                    if hook is not None:
                        hook(block, h)

    def drain(self):
        for s in range(self.n // 2):
            for d, h in self.moves(s):
                self.out(s, d, h).wait_send()


def hdot(a, b):
    return jnp.dot(a, b, precision=HIGHEST, preferred_element_type=F32)


def step_kernel(prow_ref, panel_ref, matrix_ref,
                out_ref, most_ref,
                mat, pall, slots_all, low_all, tops, staged, relay,
                from_pair, contrib, own, low_in, keys, parts,
                lower, inverse, perm, p_hi, p_lo, upper, prod,
                z_send, z_recv, r_send, r_recv, q_send, q_recv,
                one_send, one_recv, lone_send, lone_recv,
                zl_send, zl_recv, sc_send, sc_recv, local,
                pair_send, pair_recv, slot_send, slot_recv,
                lpair_send, lpair_recv, top_send, top_recv, tp_send, tp_recv,
                rl_send, rl_recv, rs_send):
    pr = lax.axis_index("prow")
    z = lax.axis_index("pcol")
    core = lax.rem(pr, 2)
    chip = pr // 2
    x = lax.rem(chip, NX)
    y = chip // NX
    rows, cols = mat.shape
    half = cols // 2

    def dev(x=x, y=y, c=core, z=z):
        return ((y * NX + x) * 2 + c, z)

    def remote(src, dst, ss, rs, device):
        return pltpu.make_async_remote_copy(
            src_ref=src, dst_ref=dst, send_sem=ss, recv_sem=rs,
            device_id=device, device_id_type=MESH)

    partner = dev(c=1 - core)
    is_root = pr == 0
    fetch = pltpu.make_async_copy(matrix_ref, mat, local.at[5])
    fetch.start()
    own_panel = pltpu.make_async_copy(panel_ref, pall.at[z], local.at[0])
    own_panel.start()
    barrier = pltpu.get_barrier_semaphore()

    def hello(device):
        pl.semaphore_signal(barrier, inc=1, device_id=device, device_id_type=MESH)

    for d in range(1, NZ):
        hello(dev(z=lax.rem(z + d, NZ)))
    for d in range(1, NX):
        hello(dev(x=lax.rem(x + d, NX)))
    for d in range(1, NY):
        hello(dev(y=lax.rem(y + d, NY)))
    hello(partner)
    near = NZ + NX + NY - 2

    @pl.when(is_root)
    def _():
        @pl.loop(1, 2 * CHIPS)
        def _(q):
            hello((q, z))

    @pl.when(jnp.logical_not(is_root))
    def _():
        hello((0, z))

    p_r = prow_ref[...]
    c_r = chip_of(p_r)
    here = c_r == chip
    before = (iota((NB, NB), 0) < iota((NB, NB), 1)).astype(BF16)
    rank = mm(jnp.broadcast_to(here.astype(BF16), (16, NB)), before)[:1].astype(I32)
    mine_at = here & (rank == iota((CAP, NB), 0))
    row = jnp.sum(jnp.where(mine_at, (p_r + 1).astype(F32), 0.0), axis=1, keepdims=True).astype(I32) - 1
    pick = (row - pr * rows) == iota((CAP, rows), 1)
    sel = (pick & (row >= NB)).astype(BF16)
    fetch.wait()
    got = select_rows(pick.astype(BF16), mat[...])
    contrib[0] = got[:, :half]
    contrib[1] = got[:, half:]
    own_panel.wait()

    @pl.when(is_root)
    def _():
        pl.semaphore_wait(barrier, near + 2 * CHIPS - 1)

    @pl.when(jnp.logical_not(is_root))
    def _():
        pl.semaphore_wait(barrier, near + 1)

    def line(mine):
        other = 1 - mine
        n1, n2 = (NX, NY) if mine == 0 else (NY, NX)
        a1, a2 = (x, y) if mine == 0 else (y, x)
        peer1 = (lambda i: dev(x=i)) if mine == 0 else (lambda i: dev(y=i))
        peer2 = (lambda i: dev(y=i)) if mine == 0 else (lambda i: dev(x=i))
        slots = slots_all.at[mine]
        lows = low_all.at[mine]
        low_root = is_root & (z < NB // 64)
        has_low = (z < NB // 64) & (lax.rem(z, 2) == mine)
        top_here = is_root if mine == 0 else (pr < 0)

        def part(ref):
            if mine == 0:
                return lambda b, h: ref.at[b, pl.ds(2 * h, 2)]
            return lambda b, h: ref.at[pl.ds(4 * h, 4), b]

        zr = Ring(NZ, z, lambda b, h: pall.at[b, pl.ds(32 * h, 32)],
                  lambda i: dev(z=i), z_send, z_recv)
        ring = Ring(n2, a2, part(slots), peer2, r_send, r_recv)
        lring = Ring(n2, a2, part(lows), peer2, q_send, q_recv)
        last = n2 // 2 - 1
        pair = lambda: remote(contrib.at[other], from_pair, pair_send, pair_recv, partner)
        keep = lambda: pltpu.make_async_copy(own, slots.at[y, x], local.at[2])
        keep_low = lambda: pltpu.make_async_copy(low_in, lows.at[y, x, z // 2], local.at[3])

        def spread(d):
            return remote(own, slots.at[y, x], one_send.at[d], one_recv.at[d],
                          peer1(lax.rem(a1 + d, n1)))

        def lspread(d):
            return remote(lows.at[y, x], lows.at[y, x], lone_send.at[d], lone_recv.at[d],
                          peer1(lax.rem(a1 + d, n1)))

        def zspread(d):
            return remote(low_in, lows.at[y, x, z // 2], zl_send.at[d], zl_recv.at[z // 2],
                          dev(z=lax.rem(z + d, NZ)))

        def spread_wait(ref, ss, rs):
            for d in range(1, n1):
                src = lax.rem(a1 + n1 - d, n1)
                dst = ref.at[y, src] if mine == 0 else ref.at[src, x]
                remote(dst, dst, ss.at[d], rs.at[d], peer1(src)).wait_recv()

        def to_pair(block, h):
            ref = part(slots)(block, h)
            remote(ref, ref, slot_send, slot_recv, partner).start()

        def seg0():
            zr.step(0)

            @pl.when(low_root)
            def _():
                @pl.loop(0, CHIPS)
                def _(q):
                    src = panel_ref.at[pl.ds(pl.multiple_of(q // NX * 8, 8), 8),
                                       pl.ds(pl.multiple_of(lax.rem(q, NX) * 128, 128), 128)]

                    @pl.when((q > 0) | (lax.rem(z, 2) == 1))
                    def _():
                        remote(src, low_in, sc_send.at[q], sc_recv,
                               (q * 2 + lax.rem(z, 2), z)).start()

            pair().start()

            @pl.when(is_root & has_low)
            def _():
                tile = pltpu.make_async_copy(panel_ref.at[pl.ds(0, 8), pl.ds(0, 128)], low_in, local.at[1])
                tile.start()
                tile.wait()

            pair().wait_recv()
            own[...] = contrib[mine] + from_pair[...]
            keep().start()
            for d in range(1, n1):
                spread(d).start()

        def seg1():
            @pl.when(has_low)
            def _():
                @pl.when(jnp.logical_not(top_here))
                def _():
                    remote(low_in, low_in, sc_send.at[0], sc_recv, partner).wait_recv()
                keep_low().start()
                for d in range(1, NZ):
                    zspread(d).start()
            zr.step(1)

        def seg2():
            keep().wait()
            spread_wait(slots, one_send, one_recv)
            ring.step(0)
            for h in (0, 1):
                to_pair(a2, h)
            zr.step(2)

        def seg3():
            for i in range(4):
                @pl.when(z != 2 * i + mine)
                def _():
                    ref = lows.at[y, x, i]
                    remote(ref, ref, zl_send.at[1], zl_recv.at[i], partner).wait_recv()

            @pl.when(has_low)
            def _():
                keep_low().wait()
            for d in range(1, n1):
                lspread(d).start()
            ring.step(1, to_pair)
            zr.step(3)

        def seg4():
            spread_wait(lows, lone_send, lone_recv)
            lring.step(0)
            if last >= 2:
                ring.step(2, to_pair)
            zr.step(4)
            lring.step(1)

        def seg5():
            if last >= 3:
                ring.step(3, to_pair)
                lring.step(2)
            zr.step(5)
            if last >= 3:
                lring.step(3)
            ring.finish(to_pair)
            if mine == 0:
                @pl.when(is_root)
                def _():
                    remote(staged.at[0, 0, 1], tops.at[1], top_send.at[0, 1], top_recv, partner).start()
                    for c in (0, 1):
                        for q in (1, 3):
                            via(q, c).start()

                    @pl.loop(1, CHIPS)
                    def _(q):
                        xx, yy = lax.rem(q, NX), q // NX

                        @pl.when((lax.rem(xx, 2) == 0) | (yy == 0))
                        def _():
                            for c in (0, 1):
                                remote(staged.at[yy, xx, c], tops.at[c], top_send.at[q, c], top_recv,
                                       (q * 2 + c, z)).start()
            zr.finish()
            ref = slots_all.at[other]
            remote(ref, ref, slot_send, slot_recv, partner).wait_recv()

        def via(q, c):
            return remote(staged.at[pl.ds(1, NY - 1), q, c], relay,
                          rl_send.at[q // 2, c], rl_recv, (q * 2 + c, z))

        def seg6():
            lring.finish()
            remote(lows, lows, lpair_send, lpair_recv, partner).start()
            ref = low_all.at[other]
            remote(ref, ref, lpair_send, lpair_recv, partner).wait_recv()

        relays = (y == 0) & (lax.rem(x, 2) == 1)

        def onward(i):
            return remote(relay.at[i], tops.at[mine], rs_send.at[i], top_recv, dev(y=i + 1))

        def seg7():
            @pl.when(relays)
            def _():
                remote(relay, relay, rl_send.at[0, 0], rl_recv, partner).wait_recv()
                for i in range(NY - 1):
                    onward(i).start()

        def tpair():
            return remote(tops.at[mine], tops.at[mine], tp_send, tp_recv, partner)

        def seg8():
            @pl.when(jnp.logical_not(top_here))
            def _():
                remote(tops.at[mine], tops.at[mine], top_send.at[0, 0], top_recv, partner).wait_recv()
            if mine == 0:
                @pl.when(is_root)
                def _():
                    first = pltpu.make_async_copy(staged.at[0, 0, 0], tops.at[0], local.at[4])
                    first.start()
                    first.wait()
            tpair().start()
            ref = tops.at[other]
            remote(ref, ref, tp_send, tp_recv, partner).wait_recv()

        def seg9():
            pair().wait_send()
            for d in range(1, n1):
                spread(d).wait_send()
                lspread(d).wait_send()
            remote(lows, lows, lpair_send, lpair_recv, partner).wait_send()
            tpair().wait_send()
            ring.drain()
            lring.drain()
            zr.drain()
            remote(slots, slots, slot_send, slot_recv, partner).wait_send()

            @pl.when(has_low)
            def _():
                for d in range(1, NZ):
                    zspread(d).wait_send()

            @pl.when(low_root & (mine == 0))
            def _():
                @pl.loop(0, CHIPS)
                def _(q):
                    @pl.when((q > 0) | (lax.rem(z, 2) == 1))
                    def _():
                        remote(low_in, low_in, sc_send.at[q], sc_recv, partner).wait_send()

            @pl.when(relays)
            def _():
                for i in range(NY - 1):
                    onward(i).wait_send()

            if mine == 0:
                @pl.when(is_root)
                def _():
                    remote(staged.at[0, 0, 1], tops.at[1], top_send.at[0, 1], top_recv, partner).wait_send()
                    for c in (0, 1):
                        for q in (1, 3):
                            via(q, c).wait_send()

                    @pl.loop(1, CHIPS)
                    def _(q):
                        xx, yy = lax.rem(q, NX), q // NX

                        @pl.when((lax.rem(xx, 2) == 0) | (yy == 0))
                        def _():
                            for c in (0, 1):
                                remote(staged.at[yy, xx, c], tops.at[c], top_send.at[q, c], top_recv,
                                       partner).wait_send()

        return [seg0, seg1, seg2, seg3, seg4, seg5, seg6, seg7, seg8, seg9]

    segments = [line(0), line(1)]

    def run(k):
        for mine in (0, 1):
            pl.when(core == mine)(segments[mine][k])

    def column(v):
        wide = jnp.broadcast_to(v.astype(F32), (128, NB)).T.astype(I32)
        return jnp.concatenate([wide] * (NB // 128), axis=1)

    def top_index():
        p_c = column(p_r)
        c_c = chip_of(p_c)
        i0, i1 = iota((NB, NB), 0), iota((NB, NB), 1)
        d_r = c_r * CAP + count((c_c == c_r) & (i0 < i1), 0)
        t_r = iota((1, NB), 1)
        left_rank = t_r - count(p_c < t_r, 0)
        chosen = count(p_c == t_r, 0) > 0
        vac_rank = count((p_c >= NB) & (p_c < p_r), 0)
        keys[0:1] = d_r
        keys[1:2] = jnp.where(chosen, -2, left_rank)
        keys[2:3] = jnp.where(p_r >= NB, vac_rank + 1, 0)
        for i, piece in enumerate(split3(mat[:NB])):
            parts[i] = piece

    def top_piece(g):
        n = 8 * CAP
        e = keys[0:1] == g * n + iota((n, NB), 0)
        key = jnp.sum(jnp.where(e, keys[2:3].astype(F32), 0.0), axis=1, keepdims=True).astype(I32) - 1
        onehot = (key == keys[1:2]).astype(BF16)
        res = (mm(onehot, parts[2]) + mm(onehot, parts[1])) + mm(onehot, parts[0])
        for c in (0, 1):
            staged[pl.ds(2 * g, 2), :, c] = res[:, c * half:c * half + half].reshape(2, NX, CAP, half)

    def on_root(*work):
        @pl.when(is_root)
        def _():
            for w in work:
                w()

    run(0)
    on_root(top_index, lambda: top_piece(0))
    run(1)
    run(2)
    on_root(lambda: top_piece(1), lambda: top_piece(2))
    p_c = column(p_r)
    c_c = chip_of(p_c)
    slot_c = jnp.sum(((c_c == c_r) & (iota((NB, NB), 1) < iota((NB, NB), 0))).astype(F32),
                     axis=1, keepdims=True)
    most_ref[0] = jnp.max(slot_c)
    dest = c_c[:, :128] * CAP + jnp.broadcast_to(slot_c.astype(I32), (NB, 128))
    for k in range(CHIPS * CAP // 128):
        perm[:, 128 * k:128 * k + 128] = (dest == iota((NB, 128), 1) + 128 * k).astype(BF16)
    run(3)
    on_root(lambda: top_piece(3))
    run(4)
    run(5)

    @pl.loop(0, 2)
    def _(n):
        upper[n] = select_rows(perm[...], slots_all[n].reshape(CHIPS * CAP, half))

    full = pall[...].reshape(rows, NB)
    hi = full.astype(BF16)
    p_hi[...] = hi
    p_lo[...] = (full - hi.astype(F32)).astype(BF16)
    run(6)
    for i in range(NB // 64):
        for yy in range(NY):
            for xx in range(NX):
                if 128 * xx < 64 * i + 64:
                    lower[64 * i + 8 * yy:64 * i + 8 * yy + 8, 128 * xx:128 * xx + 128] = (
                        low_all[i % 2, yy, xx, i // 2])
    i0, i1 = iota((128, 128), 0), iota((128, 128), 1)
    eye = (i0 == i1).astype(F32)
    diag = [lower[128 * k:128 * k + 128, 128 * k:128 * k + 128] for k in range(4)]
    size = 1
    invs = [eye] * 4
    while size < 128:
        mask = ((i0 // (2 * size)) == (i1 // (2 * size))) & (
            (i0 // size) % 2 == 1) & ((i1 // size) % 2 == 0)
        offs = [jnp.where(mask, d, 0.0) for d in diag]
        if size == 1:
            invs = [eye - o for o in offs]
        else:
            mids = [hdot(o, v) for o, v in zip(offs, invs)]
            invs = [v - hdot(v, t) for v, t in zip(invs, mids)]
        size *= 2
    for k in range(4):
        inverse[k] = invs[k]
    run(7)

    @pl.loop(0, 2)
    def _(n):
        for i in range(4):
            rhs = upper[n, 128 * i:128 * i + 128]
            if i:
                rhs = rhs - hdot(lower[128 * i:128 * i + 128, :128 * i], upper[n, :128 * i])
            upper[n, 128 * i:128 * i + 128] = hdot(inverse[i], rhs)
        u = upper[n]
        u_hi = u.astype(BF16)
        u_lo = (u - u_hi.astype(F32)).astype(BF16)
        prod[n] = (mm(p_lo[...], u_hi) + mm(p_hi[...], u_lo)) + mm(p_hi[...], u_hi)

    run(8)
    replaced = mm(sel, jnp.ones((CAP, 128), BF16), ((0,), (0,)))[:, :1] > 0.5
    for n in (0, 1):
        at = slice(n * half, n * half + half)
        incoming = select_rows(sel, tops[n], ((0,), (0,)))
        prod[n] = jnp.where(replaced, incoming, mat[:, at]) - prod[n]

        @pl.when(is_root)
        def _():
            prod[n, :NB] = upper[n]
        pltpu.make_async_copy(prod.at[n], out_ref.at[:, pl.ds(n * half, half)], local.at[6 + n]).start()
    run(9)
    for n in (0, 1):
        pltpu.make_async_copy(prod.at[n], out_ref.at[:, pl.ds(n * half, half)], local.at[6 + n]).wait()


def step(p_row, panel, matrix):
    rows, cols = matrix.shape
    half = cols // 2
    dma = pltpu.SemaphoreType.DMA
    vm = pl.BlockSpec(memory_space=pltpu.VMEM)
    anyspec = pl.BlockSpec(memory_space=pl.ANY)
    v = pltpu.VMEM
    return pl.pallas_call(
        step_kernel,
        out_shape=(
            jax.ShapeDtypeStruct((rows, cols), F32),
            jax.ShapeDtypeStruct((1,), F32),
        ),
        in_specs=[vm, vm, anyspec],
        out_specs=(anyspec, pl.BlockSpec(memory_space=pltpu.SMEM)),
        scratch_shapes=[
            v((rows, cols), F32), v((NZ,) + panel.shape, F32),
            v((2, NY, NX, CAP, half), F32), v((2, NY, NX, 4, 8, 128), F32),
            v((2, CAP, half), F32), v((NY, NX, 2, CAP, half), F32), v((NY - 1, CAP, half), F32),
            v((CAP, half), F32), v((2, CAP, half), F32), v((CAP, half), F32), v((8, 128), F32),
            v((8, NB), I32), v((3, NB, cols), BF16),
            v((NB, NB), F32), v((4, 128, 128), F32), v((NB, CHIPS * CAP), BF16),
            v((rows, NB), BF16), v((rows, NB), BF16), v((2, NB, half), F32), v((2, rows, half), F32),
            dma((2, NZ // 2, 2)), dma((2, NZ // 2, 2)),
            dma((2, NY // 2, 2)), dma((2, NY // 2, 2)),
            dma((2, NY // 2, 2)), dma((2, NY // 2, 2)),
            dma((NY,)), dma((NY,)), dma((NY,)), dma((NY,)),
            dma((NZ,)), dma((4,)), dma((CHIPS,)), dma, dma((8,)),
            dma, dma, dma, dma, dma, dma, dma((CHIPS, 2)), dma, dma, dma,
            dma((2, 2)), dma, dma((NY - 1,)),
        ],
        compiler_params=pltpu.CompilerParams(collective_id=0, has_side_effects=True),
        name="step",
    )(p_row, panel, matrix)


def ring_sum(value, axis):
    n = lax.axis_size(axis)
    pairs = [(i, (i + 1) % n) for i in range(n)]

    def body(_, carry):
        total, moving = carry
        moving = lax.ppermute(moving, axis, pairs)
        return total + moving, moving

    return lax.fori_loop(0, n - 1, body, (value, value))[0]


def dense(matrix, panel, pivot_rows):
    own_rows = matrix.shape[0]
    row = lax.axis_index("prow")
    col = lax.axis_index("pcol")
    row_base = row * own_rows
    slab = jnp.zeros((lax.axis_size("pcol"),) + panel.shape, F32)
    panels = ring_sum(lax.dynamic_update_slice(slab, panel[None], (col, 0, 0)), "pcol")
    panels = panels.reshape(own_rows, NB)
    local_rows = pivot_rows - row_base
    owned = (local_rows >= 0) & (local_rows < own_rows)
    picked = (local_rows[:, None] == jnp.arange(own_rows, dtype=I32)[None, :]).astype(F32)
    picked = jnp.dot(picked, matrix, precision=HIGHEST, preferred_element_type=F32)
    first = jnp.where(row == 0, 1.0, 0.0)
    pack = jnp.concatenate([picked, matrix[:NB] * first], axis=1)
    pack = jnp.concatenate([pack, panels[:NB] * first], axis=1)
    pack = ring_sum(pack, "prow")
    own_cols = matrix.shape[1]
    new_top, top_rows, lower = pack[:, :own_cols], pack[:, own_cols:2 * own_cols], pack[:, 2 * own_cols:]

    def solve_row(j, upper):
        coef = lax.dynamic_slice(lower, (j, 0), (1, NB))
        coef = jnp.where(jnp.arange(NB)[None, :] < j, coef, 0.0)
        done = jnp.dot(coef, upper, precision=HIGHEST, preferred_element_type=F32)
        mine = lax.dynamic_slice(upper, (j, 0), (1, own_cols)) - done
        return lax.dynamic_update_slice(upper, mine, (j, 0))

    upper = lax.fori_loop(0, NB, solve_row, new_top)
    vacated = pivot_rows >= NB
    top_index = jnp.arange(NB, dtype=I32)
    chosen = jnp.any(pivot_rows[None, :] == top_index[:, None], axis=1)
    left_rank = top_index - jnp.sum((pivot_rows[None, :] < top_index[:, None]).astype(I32), axis=1)
    vac_rank = jnp.sum((vacated[None, :] & (pivot_rows[None, :] < pivot_rows[:, None])).astype(I32), axis=1)
    pairing = (vacated[:, None] & jnp.logical_not(chosen)[None, :]
               & (left_rank[None, :] == vac_rank[:, None])).astype(F32)
    incoming = jnp.dot(pairing, top_rows, precision=HIGHEST, preferred_element_type=F32)
    global_rows = row_base + jnp.arange(own_rows, dtype=I32)
    place = (global_rows[:, None] == pivot_rows[None, :]) & vacated[None, :]
    moved = jnp.dot(place.astype(F32), incoming, precision=HIGHEST, preferred_element_type=F32)
    swapped = jnp.where(jnp.any(place, axis=1)[:, None], moved, matrix)
    updated = swapped - jnp.dot(panels, upper, precision=HIGHEST, preferred_element_type=F32)
    top_fill = jnp.pad(upper, ((0, own_rows - NB), (0, 0)))
    return jnp.where((global_rows < NB)[:, None], top_fill, updated)


def shards(matrix, panel, pivot_rows):
    out, most = step(pivot_rows.reshape(1, NB), panel, matrix)
    return lax.cond(most[0] < CAP, lambda: out, lambda: dense(matrix, panel, pivot_rows))


def solution(mesh):
    return jax.shard_map(
        shards,
        mesh=mesh,
        in_specs=(P("prow", "pcol"), P(("prow", "pcol"), None), P()),
        out_specs=P("prow", "pcol"),
        check_vma=False,
    )
```

```python
import functools

import jax
import jax.numpy as jnp
from jax import lax
from jax.experimental import pallas as pl
from jax.experimental.pallas import tpu as pltpu
from jax.sharding import PartitionSpec as P

NB = 512
NX, NY, NZ = 4, 8, 12
CHIPS = NX * NY
CAP = 32
MESH = pl.DeviceIdType.MESH
F32, BF16, I32 = jnp.float32, jnp.bfloat16, jnp.int32
HIGHEST = lax.Precision.HIGHEST


def mm(a, b, dims=((1,), (0,))):
    return lax.dot_general(a, b, (dims, ((), ())), preferred_element_type=F32)


def split3(v):
    hi = v.astype(BF16)
    rest = v - hi.astype(F32)
    mid = rest.astype(BF16)
    low = (rest - mid.astype(F32)).astype(BF16)
    return hi, mid, low


def select_rows(onehot, v, dims=((1,), (0,))):
    hi, mid, low = split3(v)
    return (mm(onehot, low, dims) + mm(onehot, mid, dims)) + mm(onehot, hi, dims)


def iota(shape, axis):
    return lax.broadcasted_iota(I32, shape, axis)


def chip_of(rows):
    return ((rows >> 9) * 171) >> 9


def count(mask, axis):
    return jnp.sum(mask.astype(F32), axis=axis, keepdims=True).astype(I32)


class Ring:
    def __init__(self, n, me, piece, device, send, recv):
        self.n, self.me, self.piece, self.device = n, me, piece, device
        self.send, self.recv = send, recv
        self.waited = set()

    def moves(self, s):
        last = s == self.n // 2 - 1
        return [(d, h) for h in (0, 1) for d in (0, 1) if not (last and d != h)]

    def copy(self, s, d, h, block):
        n = self.n
        ref = self.piece(lax.rem(block + 2 * n, n), h)
        peer = lax.rem(self.me + (1 if d == 0 else n - 1), n)
        return pltpu.make_async_remote_copy(
            src_ref=ref, dst_ref=ref,
            send_sem=self.send.at[d, s, h], recv_sem=self.recv.at[d, s, h],
            device_id=self.device(peer), device_id_type=MESH)

    def out(self, s, d, h):
        return self.copy(s, d, h, self.me - s if d == 0 else self.me + s)

    def arrive(self, s, d, h):
        block = self.me - 1 - s if d == 0 else self.me + 1 + s
        self.copy(s, d, h, block).wait_recv()
        self.waited.add((s, d, h))
        return lax.rem(block + 2 * self.n, self.n)

    def step(self, s, hook=None):
        for d, h in self.moves(s):
            if s > 0:
                block = self.arrive(s - 1, d, h)
                if hook is not None:
                    hook(block, h)
            self.out(s, d, h).start()

    def finish(self, hook=None):
        for s in range(self.n // 2):
            for d, h in self.moves(s):
                if (s, d, h) not in self.waited:
                    block = self.arrive(s, d, h)
                    if hook is not None:
                        hook(block, h)

    def drain(self):
        for s in range(self.n // 2):
            for d, h in self.moves(s):
                self.out(s, d, h).wait_send()


def hdot(a, b):
    return jnp.dot(a, b, precision=HIGHEST, preferred_element_type=F32)


def halves_inverse(diag, size_to):
    i0, i1 = iota(diag.shape, 0), iota(diag.shape, 1)
    inv = (i0 == i1).astype(F32)
    size = 1
    while size < size_to:
        mask = ((i0 // (2 * size)) == (i1 // (2 * size))) & (
            (i0 // size) % 2 == 1) & ((i1 // size) % 2 == 0)
        off = jnp.where(mask, diag, 0.0)
        inv = inv - (off if size == 1 else hdot(inv, hdot(off, inv)))
        size *= 2
    return inv


def step_kernel(prow_ref, panel_ref, matrix_ref,
                u_ref, p_ref, tops_ref, sel_ref, most_ref,
                mat, pall, slots_all, low_all, tops, staged, relay,
                from_pair, contrib, own, low_in, keys, parts,
                low_src, lower, inverse, perm, upper, sel,
                z_send, z_recv, r_send, r_recv, q_send, q_recv,
                one_send, one_recv, lone_send, lone_recv,
                zl_send, zl_recv, sc_send, sc_recv, local,
                pair_send, pair_recv, slot_send, slot_recv,
                lpair_send, lpair_recv, top_send, top_recv, tp_send, tp_recv,
                rl_send, rl_recv, rs_send):
    pr = lax.axis_index("prow")
    z = lax.axis_index("pcol")
    core = lax.rem(pr, 2)
    chip = pr // 2
    x = lax.rem(chip, NX)
    y = chip // NX
    rows, cols = mat.shape
    half = cols // 2

    def dev(x=x, y=y, c=core, z=z):
        return ((y * NX + x) * 2 + c, z)

    def remote(src, dst, ss, rs, device):
        return pltpu.make_async_remote_copy(
            src_ref=src, dst_ref=dst, send_sem=ss, recv_sem=rs,
            device_id=device, device_id_type=MESH)

    partner = dev(c=1 - core)
    is_root = pr == 0
    fetch = pltpu.make_async_copy(matrix_ref, mat, local.at[5])
    fetch.start()
    own_panel = pltpu.make_async_copy(panel_ref, pall.at[z], local.at[0])
    own_panel.start()
    barrier = pltpu.get_barrier_semaphore()

    def hello(device):
        pl.semaphore_signal(barrier, inc=1, device_id=device, device_id_type=MESH)

    for d in range(1, NZ):
        hello(dev(z=lax.rem(z + d, NZ)))
    for d in range(1, NX):
        hello(dev(x=lax.rem(x + d, NX)))
    for d in range(1, NY):
        hello(dev(y=lax.rem(y + d, NY)))
    hello(partner)
    near = NZ + NX + NY - 2

    @pl.when(is_root)
    def _():
        @pl.loop(1, 2 * CHIPS)
        def _(q):
            hello((q, z))

    @pl.when(jnp.logical_not(is_root))
    def _():
        hello((0, z))

    p_r = prow_ref[...]
    c_r = chip_of(p_r)
    here = c_r == chip
    before = (iota((NB, NB), 0) < iota((NB, NB), 1)).astype(BF16)
    rank = mm(jnp.broadcast_to(here.astype(BF16), (16, NB)), before)[:1].astype(I32)
    mine_at = here & (rank == iota((CAP, NB), 0))
    row = jnp.sum(jnp.where(mine_at, (p_r + 1).astype(F32), 0.0), axis=1, keepdims=True).astype(I32) - 1
    pick = (row - pr * rows) == iota((CAP, rows), 1)
    sel[...] = (pick & (row >= NB)).astype(F32)
    keep_sel = pltpu.make_async_copy(sel, sel_ref, local.at[6])
    fetch.wait()
    got = select_rows(pick.astype(BF16), mat[...])
    contrib[0] = got[:, :half]
    contrib[1] = got[:, half:]
    own_panel.wait()

    @pl.when(is_root & (z < NB // 64))
    def _():
        at = iota((64, NB), 1) == iota((64, NB), 0) + 64 * z
        pan = panel_ref[...]
        hi, mid, low = split3(pan)
        onto = at.astype(BF16)
        to = ((1,), (1,))
        diag = (mm(low, onto, to) + mm(mid, onto, to)) + mm(hi, onto, to)
        inv = halves_inverse(diag, 64)
        hi, mid, low = split3(inv)
        back = (mm(low, onto) + mm(mid, onto)) + mm(hi, onto)
        col = iota((64, NB), 1)
        low_src[...] = jnp.where((col >= 64 * z) & (col < 64 * z + 64), back, pan)

    @pl.when(is_root)
    def _():
        pl.semaphore_wait(barrier, near + 2 * CHIPS - 1)

    @pl.when(jnp.logical_not(is_root))
    def _():
        pl.semaphore_wait(barrier, near + 1)

    def line(mine):
        other = 1 - mine
        n1, n2 = (NX, NY) if mine == 0 else (NY, NX)
        a1, a2 = (x, y) if mine == 0 else (y, x)
        peer1 = (lambda i: dev(x=i)) if mine == 0 else (lambda i: dev(y=i))
        peer2 = (lambda i: dev(y=i)) if mine == 0 else (lambda i: dev(x=i))
        slots = slots_all.at[mine]
        lows = low_all.at[mine]
        low_root = is_root & (z < NB // 64)
        has_low = (z < NB // 64) & (lax.rem(z, 2) == mine)
        top_here = is_root if mine == 0 else (pr < 0)

        def part(ref):
            if mine == 0:
                return lambda b, h: ref.at[b, pl.ds(2 * h, 2)]
            return lambda b, h: ref.at[pl.ds(4 * h, 4), b]

        zr = Ring(NZ, z, lambda b, h: pall.at[b, pl.ds(32 * h, 32)],
                  lambda i: dev(z=i), z_send, z_recv)
        ring = Ring(n2, a2, part(slots), peer2, r_send, r_recv)
        lring = Ring(n2, a2, part(lows), peer2, q_send, q_recv)
        last = n2 // 2 - 1
        pair = lambda: remote(contrib.at[other], from_pair, pair_send, pair_recv, partner)
        keep = lambda: pltpu.make_async_copy(own, slots.at[y, x], local.at[2])
        keep_low = lambda: pltpu.make_async_copy(low_in, lows.at[y, x, z // 2], local.at[3])

        def spread(d):
            return remote(own, slots.at[y, x], one_send.at[d], one_recv.at[d],
                          peer1(lax.rem(a1 + d, n1)))

        def lspread(d):
            return remote(lows.at[y, x], lows.at[y, x], lone_send.at[d], lone_recv.at[d],
                          peer1(lax.rem(a1 + d, n1)))

        def zspread(d):
            return remote(low_in, lows.at[y, x, z // 2], zl_send.at[d], zl_recv.at[z // 2],
                          dev(z=lax.rem(z + d, NZ)))

        def spread_wait(ref, ss, rs):
            for d in range(1, n1):
                src = lax.rem(a1 + n1 - d, n1)
                dst = ref.at[y, src] if mine == 0 else ref.at[src, x]
                remote(dst, dst, ss.at[d], rs.at[d], peer1(src)).wait_recv()

        def to_pair(block, h):
            ref = part(slots)(block, h)
            remote(ref, ref, slot_send, slot_recv, partner).start()

        def seg0():
            zr.step(0)

            @pl.when(low_root)
            def _():
                @pl.loop(0, CHIPS)
                def _(q):
                    src = low_src.at[pl.ds(pl.multiple_of(q // NX * 8, 8), 8),
                                       pl.ds(pl.multiple_of(lax.rem(q, NX) * 128, 128), 128)]

                    @pl.when((q > 0) | (lax.rem(z, 2) == 1))
                    def _():
                        remote(src, low_in, sc_send.at[q], sc_recv,
                               (q * 2 + lax.rem(z, 2), z)).start()

            pair().start()

            @pl.when(is_root & has_low)
            def _():
                tile = pltpu.make_async_copy(low_src.at[pl.ds(0, 8), pl.ds(0, 128)], low_in, local.at[1])
                tile.start()
                tile.wait()

            pair().wait_recv()
            own[...] = contrib[mine] + from_pair[...]
            keep().start()
            for d in range(1, n1):
                spread(d).start()

        def seg1():
            @pl.when(has_low)
            def _():
                @pl.when(jnp.logical_not(top_here))
                def _():
                    remote(low_in, low_in, sc_send.at[0], sc_recv, partner).wait_recv()
                keep_low().start()
                for d in range(1, NZ):
                    zspread(d).start()
            zr.step(1)

        def seg2():
            zr.step(2)
            for i in range(4):
                @pl.when(z != 2 * i + mine)
                def _():
                    ref = lows.at[y, x, i]
                    remote(ref, ref, zl_send.at[1], zl_recv.at[i], partner).wait_recv()

            @pl.when(has_low)
            def _():
                keep_low().wait()
            for d in range(1, n1):
                lspread(d).start()
            keep().wait()
            spread_wait(slots, one_send, one_recv)
            ring.step(0)
            for h in (0, 1):
                to_pair(a2, h)

        def seg3():
            zr.step(3)
            spread_wait(lows, lone_send, lone_recv)
            lring.step(0)
            ring.step(1, to_pair)

        def seg4():
            zr.step(4)
            lring.step(1)
            if last >= 2:
                ring.step(2, to_pair)

        def seg5():
            zr.step(5)
            if last >= 3:
                lring.step(2)
                ring.step(3, to_pair)
                lring.step(3)
            ring.finish(to_pair)
            if mine == 0:
                @pl.when(is_root)
                def _():
                    remote(staged.at[0, 0, 1], tops.at[1], top_send.at[0, 1], top_recv, partner).start()
                    for c in (0, 1):
                        for q in (1, 3):
                            via(q, c).start()

                    @pl.loop(1, CHIPS)
                    def _(q):
                        xx, yy = lax.rem(q, NX), q // NX

                        @pl.when((lax.rem(xx, 2) == 0) | (yy == 0))
                        def _():
                            for c in (0, 1):
                                remote(staged.at[yy, xx, c], tops.at[c], top_send.at[q, c], top_recv,
                                       (q * 2 + c, z)).start()
            zr.finish()
            lring.finish()
            remote(lows, lows, lpair_send, lpair_recv, partner).start()
            ref = slots_all.at[other]
            remote(ref, ref, slot_send, slot_recv, partner).wait_recv()

        def via(q, c):
            return remote(staged.at[pl.ds(1, NY - 1), q, c], relay,
                          rl_send.at[q // 2, c], rl_recv, (q * 2 + c, z))

        def seg6():
            ref = low_all.at[other]
            remote(ref, ref, lpair_send, lpair_recv, partner).wait_recv()

        relays = (y == 0) & (lax.rem(x, 2) == 1)

        def onward(i):
            return remote(relay.at[i], tops.at[mine], rs_send.at[i], top_recv, dev(y=i + 1))

        def seg7():
            @pl.when(relays)
            def _():
                remote(relay, relay, rl_send.at[0, 0], rl_recv, partner).wait_recv()
                for i in range(NY - 1):
                    onward(i).start()

        def tpair():
            return remote(tops.at[mine], tops.at[mine], tp_send, tp_recv, partner)

        def seg8():
            @pl.when(jnp.logical_not(top_here))
            def _():
                remote(tops.at[mine], tops.at[mine], top_send.at[0, 0], top_recv, partner).wait_recv()
            if mine == 0:
                @pl.when(is_root)
                def _():
                    first = pltpu.make_async_copy(staged.at[0, 0, 0], tops.at[0], local.at[4])
                    first.start()
                    first.wait()
            tpair().start()
            ref = tops.at[other]
            remote(ref, ref, tp_send, tp_recv, partner).wait_recv()

        def seg9():
            pair().wait_send()
            for d in range(1, n1):
                spread(d).wait_send()
                lspread(d).wait_send()
            remote(lows, lows, lpair_send, lpair_recv, partner).wait_send()
            tpair().wait_send()
            ring.drain()
            lring.drain()
            zr.drain()
            remote(slots, slots, slot_send, slot_recv, partner).wait_send()

            @pl.when(has_low)
            def _():
                for d in range(1, NZ):
                    zspread(d).wait_send()

            @pl.when(low_root & (mine == 0))
            def _():
                @pl.loop(0, CHIPS)
                def _(q):
                    @pl.when((q > 0) | (lax.rem(z, 2) == 1))
                    def _():
                        remote(low_in, low_in, sc_send.at[q], sc_recv, partner).wait_send()

            @pl.when(relays)
            def _():
                for i in range(NY - 1):
                    onward(i).wait_send()

            if mine == 0:
                @pl.when(is_root)
                def _():
                    remote(staged.at[0, 0, 1], tops.at[1], top_send.at[0, 1], top_recv, partner).wait_send()
                    for c in (0, 1):
                        for q in (1, 3):
                            via(q, c).wait_send()

                    @pl.loop(1, CHIPS)
                    def _(q):
                        xx, yy = lax.rem(q, NX), q // NX

                        @pl.when((lax.rem(xx, 2) == 0) | (yy == 0))
                        def _():
                            for c in (0, 1):
                                remote(staged.at[yy, xx, c], tops.at[c], top_send.at[q, c], top_recv,
                                       partner).wait_send()

        return [seg0, seg1, seg2, seg3, seg4, seg5, seg6, seg7, seg8, seg9]

    segments = [line(0), line(1)]

    def run(k):
        for mine in (0, 1):
            pl.when(core == mine)(segments[mine][k])

    def column(v):
        wide = jnp.broadcast_to(v.astype(F32), (128, NB)).T.astype(I32)
        return jnp.concatenate([wide] * (NB // 128), axis=1)

    def top_index():
        p_c = column(p_r)
        c_c = chip_of(p_c)
        i0, i1 = iota((NB, NB), 0), iota((NB, NB), 1)
        d_r = c_r * CAP + count((c_c == c_r) & (i0 < i1), 0)
        t_r = iota((1, NB), 1)
        left_rank = t_r - count(p_c < t_r, 0)
        chosen = count(p_c == t_r, 0) > 0
        vac_rank = count((p_c >= NB) & (p_c < p_r), 0)
        keys[0:1] = d_r
        keys[1:2] = jnp.where(chosen, -2, left_rank)
        keys[2:3] = jnp.where(p_r >= NB, vac_rank + 1, 0)
        for i, piece in enumerate(split3(mat[:NB])):
            parts[i] = piece

    def top_piece(g):
        n = 8 * CAP
        e = keys[0:1] == g * n + iota((n, NB), 0)
        key = jnp.sum(jnp.where(e, keys[2:3].astype(F32), 0.0), axis=1, keepdims=True).astype(I32) - 1
        onehot = (key == keys[1:2]).astype(BF16)
        res = (mm(onehot, parts[2]) + mm(onehot, parts[1])) + mm(onehot, parts[0])
        for c in (0, 1):
            staged[pl.ds(2 * g, 2), :, c] = res[:, c * half:c * half + half].reshape(2, NX, CAP, half)

    def on_root(*work):
        @pl.when(is_root)
        def _():
            for w in work:
                w()

    run(0)
    keep_sel.start()
    on_root(top_index, lambda: top_piece(0))
    run(1)
    run(2)
    on_root(lambda: top_piece(1), lambda: top_piece(2))
    p_c = column(p_r)
    c_c = chip_of(p_c)
    slot_c = jnp.sum(((c_c == c_r) & (iota((NB, NB), 1) < iota((NB, NB), 0))).astype(F32),
                     axis=1, keepdims=True)
    most_ref[0] = jnp.max(slot_c)
    dest = c_c[:, :128] * CAP + jnp.broadcast_to(slot_c.astype(I32), (NB, 128))
    for k in range(CHIPS * CAP // 128):
        perm[:, 128 * k:128 * k + 128] = (dest == iota((NB, 128), 1) + 128 * k).astype(BF16)
    run(3)
    on_root(lambda: top_piece(3))
    run(4)
    run(5)
    keep_panel = pltpu.make_async_copy(pall, p_ref, local.at[7])
    keep_panel.start()
    for n in (0, 1):
        upper[:, n * half:n * half + half] = select_rows(
            perm[...], slots_all[n].reshape(CHIPS * CAP, half))
    run(6)
    for i in range(NB // 64):
        for yy in range(NY):
            for xx in range(NX):
                if 128 * xx < 64 * i + 64:
                    lower[64 * i + 8 * yy:64 * i + 8 * yy + 8, 128 * xx:128 * xx + 128] = (
                        low_all[i % 2, yy, xx, i // 2])
    i0, i1 = iota((128, 128), 0), iota((128, 128), 1)
    for k in range(4):
        block = lower[128 * k:128 * k + 128, 128 * k:128 * k + 128]
        two = jnp.where((i0 // 64) == (i1 // 64), block, 0.0)
        off = jnp.where(i0 // 64 > i1 // 64, block, 0.0)
        inverse[k] = two - hdot(two, hdot(off, two))
    run(7)

    def keep_upper(i):
        return pltpu.make_async_copy(upper.at[pl.ds(128 * i, 128)], u_ref.at[pl.ds(128 * i, 128)],
                                     local.at[8 + i])

    for i in range(4):
        rhs = upper[128 * i:128 * i + 128]
        if i:
            rhs = rhs - hdot(lower[128 * i:128 * i + 128, :128 * i], upper[:128 * i])
        upper[128 * i:128 * i + 128] = hdot(inverse[i], rhs)
        keep_upper(i).start()
    run(8)
    keep_tops = pltpu.make_async_copy(tops, tops_ref, local.at[12])
    keep_tops.start()
    run(9)
    keep_tops.wait()
    keep_sel.wait()
    keep_panel.wait()
    for i in range(4):
        keep_upper(i).wait()


def step(p_row, panel, matrix):
    rows, cols = matrix.shape
    half = cols // 2
    dma = pltpu.SemaphoreType.DMA
    vm = pl.BlockSpec(memory_space=pltpu.VMEM)
    anyspec = pl.BlockSpec(memory_space=pl.ANY)
    v = pltpu.VMEM
    return pl.pallas_call(
        step_kernel,
        out_shape=(
            jax.ShapeDtypeStruct((NB, cols), F32),
            jax.ShapeDtypeStruct((NZ,) + panel.shape, F32),
            jax.ShapeDtypeStruct((2, CAP, half), F32),
            jax.ShapeDtypeStruct((CAP, rows), F32),
            jax.ShapeDtypeStruct((1,), F32),
        ),
        in_specs=[vm, vm, anyspec],
        out_specs=(anyspec,) * 4 + (pl.BlockSpec(memory_space=pltpu.SMEM),),
        scratch_shapes=[
            v((rows, cols), F32), v((NZ,) + panel.shape, F32),
            v((2, NY, NX, CAP, half), F32), v((2, NY, NX, 4, 8, 128), F32),
            v((2, CAP, half), F32), v((NY, NX, 2, CAP, half), F32), v((NY - 1, CAP, half), F32),
            v((CAP, half), F32), v((2, CAP, half), F32), v((CAP, half), F32), v((8, 128), F32),
            v((8, NB), I32), v((3, NB, cols), BF16),
            v((64, NB), F32), v((NB, NB), F32), v((4, 128, 128), F32), v((NB, CHIPS * CAP), BF16),
            v((NB, cols), F32), v((CAP, rows), F32),
            dma((2, NZ // 2, 2)), dma((2, NZ // 2, 2)),
            dma((2, NY // 2, 2)), dma((2, NY // 2, 2)),
            dma((2, NY // 2, 2)), dma((2, NY // 2, 2)),
            dma((NY,)), dma((NY,)), dma((NY,)), dma((NY,)),
            dma((NZ,)), dma((4,)), dma((CHIPS,)), dma, dma((13,)),
            dma, dma, dma, dma, dma, dma, dma((CHIPS, 2)), dma, dma, dma,
            dma((2, 2)), dma, dma((NY - 1,)),
        ],
        compiler_params=pltpu.CompilerParams(collective_id=0, has_side_effects=True),
        name="step",
    )(p_row, panel, matrix)


def update_kernel(me_ref, m_ref, p_ref, u_ref, tops_ref, sel_ref, out_ref, u_hi, u_lo):
    i = pl.program_id(0)
    half = tops_ref.shape[2]
    block = out_ref.shape[0]

    @pl.when(i == 0)
    def _():
        u = u_ref[...]
        hi = u.astype(BF16)
        u_hi[...] = hi
        u_lo[...] = (u - hi.astype(F32)).astype(BF16)

    p = p_ref[...]
    p_hi = p.astype(BF16)
    p_lo = (p - p_hi.astype(F32)).astype(BF16)
    product = (mm(p_lo, u_hi[...]) + mm(p_hi, u_lo[...])) + mm(p_hi, u_hi[...])
    sel = sel_ref[...].astype(BF16)
    replaced = mm(sel, jnp.ones((CAP, 128), BF16), ((0,), (0,)))[:, :1] > 0.5
    incoming = jnp.concatenate([select_rows(sel, tops_ref[n], ((0,), (0,))) for n in (0, 1)], axis=1)
    out_ref[...] = jnp.where(replaced, incoming, m_ref[...]) - product

    @pl.when((me_ref[0] == 0) & (i < NB // block))
    def _():
        out_ref[...] = u_ref[pl.ds(i * block, block)]


def update(me, matrix, pall, upper, tops, sel):
    rows, cols = matrix.shape
    block = 256
    whole = lambda shape: pl.BlockSpec(shape, lambda n: (0,) * len(shape))
    return pl.pallas_call(
        update_kernel,
        grid=(rows // block,),
        out_shape=jax.ShapeDtypeStruct(matrix.shape, F32),
        in_specs=[
            pl.BlockSpec(memory_space=pltpu.SMEM),
            pl.BlockSpec((block, cols), lambda n: (n, 0)),
            pl.BlockSpec((block, NB), lambda n: (n, 0)),
            whole(upper.shape), whole(tops.shape),
            pl.BlockSpec((CAP, block), lambda n: (0, n)),
        ],
        out_specs=pl.BlockSpec((block, cols), lambda n: (n, 0)),
        scratch_shapes=[pltpu.VMEM((NB, cols), BF16), pltpu.VMEM((NB, cols), BF16)],
        name="update",
    )(me, matrix, pall.reshape(rows, NB), upper, tops, sel)


def ring_sum(value, axis):
    n = lax.axis_size(axis)
    pairs = [(i, (i + 1) % n) for i in range(n)]

    def body(_, carry):
        total, moving = carry
        moving = lax.ppermute(moving, axis, pairs)
        return total + moving, moving

    return lax.fori_loop(0, n - 1, body, (value, value))[0]


def dense(matrix, panel, pivot_rows):
    own_rows = matrix.shape[0]
    row = lax.axis_index("prow")
    col = lax.axis_index("pcol")
    row_base = row * own_rows
    slab = jnp.zeros((lax.axis_size("pcol"),) + panel.shape, F32)
    panels = ring_sum(lax.dynamic_update_slice(slab, panel[None], (col, 0, 0)), "pcol")
    panels = panels.reshape(own_rows, NB)
    local_rows = pivot_rows - row_base
    owned = (local_rows >= 0) & (local_rows < own_rows)
    picked = (local_rows[:, None] == jnp.arange(own_rows, dtype=I32)[None, :]).astype(F32)
    picked = jnp.dot(picked, matrix, precision=HIGHEST, preferred_element_type=F32)
    first = jnp.where(row == 0, 1.0, 0.0)
    pack = jnp.concatenate([picked, matrix[:NB] * first], axis=1)
    pack = jnp.concatenate([pack, panels[:NB] * first], axis=1)
    pack = ring_sum(pack, "prow")
    own_cols = matrix.shape[1]
    new_top, top_rows, lower = pack[:, :own_cols], pack[:, own_cols:2 * own_cols], pack[:, 2 * own_cols:]

    def solve_row(j, upper):
        coef = lax.dynamic_slice(lower, (j, 0), (1, NB))
        coef = jnp.where(jnp.arange(NB)[None, :] < j, coef, 0.0)
        done = jnp.dot(coef, upper, precision=HIGHEST, preferred_element_type=F32)
        mine = lax.dynamic_slice(upper, (j, 0), (1, own_cols)) - done
        return lax.dynamic_update_slice(upper, mine, (j, 0))

    upper = lax.fori_loop(0, NB, solve_row, new_top)
    vacated = pivot_rows >= NB
    top_index = jnp.arange(NB, dtype=I32)
    chosen = jnp.any(pivot_rows[None, :] == top_index[:, None], axis=1)
    left_rank = top_index - jnp.sum((pivot_rows[None, :] < top_index[:, None]).astype(I32), axis=1)
    vac_rank = jnp.sum((vacated[None, :] & (pivot_rows[None, :] < pivot_rows[:, None])).astype(I32), axis=1)
    pairing = (vacated[:, None] & jnp.logical_not(chosen)[None, :]
               & (left_rank[None, :] == vac_rank[:, None])).astype(F32)
    incoming = jnp.dot(pairing, top_rows, precision=HIGHEST, preferred_element_type=F32)
    global_rows = row_base + jnp.arange(own_rows, dtype=I32)
    place = (global_rows[:, None] == pivot_rows[None, :]) & vacated[None, :]
    moved = jnp.dot(place.astype(F32), incoming, precision=HIGHEST, preferred_element_type=F32)
    swapped = jnp.where(jnp.any(place, axis=1)[:, None], moved, matrix)
    updated = swapped - jnp.dot(panels, upper, precision=HIGHEST, preferred_element_type=F32)
    top_fill = jnp.pad(upper, ((0, own_rows - NB), (0, 0)))
    return jnp.where((global_rows < NB)[:, None], top_fill, updated)


def shards(matrix, panel, pivot_rows):
    me = lax.axis_index("prow").reshape(1)
    upper, pall, tops, sel, most = step(pivot_rows.reshape(1, NB), panel, matrix)
    return lax.cond(most[0] < CAP,
                    lambda: update(me, matrix, pall, upper, tops, sel),
                    lambda: dense(matrix, panel, pivot_rows))


def solution(mesh):
    return jax.shard_map(
        shards,
        mesh=mesh,
        in_specs=(P("prow", "pcol"), P(("prow", "pcol"), None), P()),
        out_specs=P("prow", "pcol"),
        check_vma=False,
    )
```

```python
import functools

import jax
import jax.numpy as jnp
from jax import lax
from jax.experimental import pallas as pl
from jax.experimental.pallas import tpu as pltpu
from jax.sharding import PartitionSpec as P

NB = 512
NX, NY, NZ = 4, 8, 12
CHIPS = NX * NY
CAP = 32
MESH = pl.DeviceIdType.MESH
F32, BF16, I32 = jnp.float32, jnp.bfloat16, jnp.int32
HIGHEST = lax.Precision.HIGHEST


def mm(a, b, dims=((1,), (0,))):
    return lax.dot_general(a, b, (dims, ((), ())), preferred_element_type=F32)


def split3(v):
    hi = v.astype(BF16)
    rest = v - hi.astype(F32)
    mid = rest.astype(BF16)
    low = (rest - mid.astype(F32)).astype(BF16)
    return hi, mid, low


def select_rows(onehot, v, dims=((1,), (0,))):
    hi, mid, low = split3(v)
    return (mm(onehot, low, dims) + mm(onehot, mid, dims)) + mm(onehot, hi, dims)


def iota(shape, axis):
    return lax.broadcasted_iota(I32, shape, axis)


def chip_of(rows):
    return ((rows >> 9) * 171) >> 9


def count(mask, axis):
    return jnp.sum(mask.astype(F32), axis=axis, keepdims=True).astype(I32)


class Ring:
    def __init__(self, n, me, piece, device, send, recv):
        self.n, self.me, self.piece, self.device = n, me, piece, device
        self.send, self.recv = send, recv
        self.waited = set()

    def moves(self, s):
        last = s == self.n // 2 - 1
        return [(d, h) for h in (0, 1) for d in (0, 1) if not (last and d != h)]

    def copy(self, s, d, h, block):
        n = self.n
        ref = self.piece(lax.rem(block + 2 * n, n), h)
        peer = lax.rem(self.me + (1 if d == 0 else n - 1), n)
        return pltpu.make_async_remote_copy(
            src_ref=ref, dst_ref=ref,
            send_sem=self.send.at[d, s, h], recv_sem=self.recv.at[d, s, h],
            device_id=self.device(peer), device_id_type=MESH)

    def out(self, s, d, h):
        return self.copy(s, d, h, self.me - s if d == 0 else self.me + s)

    def arrive(self, s, d, h):
        block = self.me - 1 - s if d == 0 else self.me + 1 + s
        self.copy(s, d, h, block).wait_recv()
        self.waited.add((s, d, h))
        return lax.rem(block + 2 * self.n, self.n)

    def step(self, s, hook=None):
        for d, h in self.moves(s):
            if s > 0:
                block = self.arrive(s - 1, d, h)
                if hook is not None:
                    hook(block, h)
            self.out(s, d, h).start()

    def finish(self, hook=None):
        for s in range(self.n // 2):
            for d, h in self.moves(s):
                if (s, d, h) not in self.waited:
                    block = self.arrive(s, d, h)
                    if hook is not None:
                        hook(block, h)

    def drain(self):
        for s in range(self.n // 2):
            for d, h in self.moves(s):
                self.out(s, d, h).wait_send()


def hdot(a, b):
    return jnp.dot(a, b, precision=HIGHEST, preferred_element_type=F32)


def halves_inverse(diag, size_to):
    i0, i1 = iota(diag.shape, 0), iota(diag.shape, 1)
    inv = (i0 == i1).astype(F32)
    size = 1
    while size < size_to:
        mask = ((i0 // (2 * size)) == (i1 // (2 * size))) & (
            (i0 // size) % 2 == 1) & ((i1 // size) % 2 == 0)
        off = jnp.where(mask, diag, 0.0)
        inv = inv - (off if size == 1 else hdot(inv, hdot(off, inv)))
        size *= 2
    return inv


def step_kernel(prow_ref, panel_ref, matrix_ref,
                u_ref, p_ref, tops_ref, sel_ref, most_ref,
                mat, pall, slots_all, low_all, tops, staged, relay,
                from_pair, contrib, own, low_in, keys, parts,
                low_src, lower, inverse, perm, upper, sel,
                z_send, z_recv, r_send, r_recv, q_send, q_recv,
                one_send, one_recv, lone_send, lone_recv,
                zl_send, zl_recv, sc_send, sc_recv, local,
                pair_send, pair_recv, slot_send, slot_recv,
                lpair_send, lpair_recv, top_send, top_recv, tp_send, tp_recv,
                rl_send, rl_recv, rs_send):
    pr = lax.axis_index("prow")
    z = lax.axis_index("pcol")
    core = lax.rem(pr, 2)
    chip = pr // 2
    x = lax.rem(chip, NX)
    y = chip // NX
    rows, cols = mat.shape
    half = cols // 2

    def dev(x=x, y=y, c=core, z=z):
        return ((y * NX + x) * 2 + c, z)

    def remote(src, dst, ss, rs, device):
        return pltpu.make_async_remote_copy(
            src_ref=src, dst_ref=dst, send_sem=ss, recv_sem=rs,
            device_id=device, device_id_type=MESH)

    partner = dev(c=1 - core)
    is_root = pr == 0
    fetch = pltpu.make_async_copy(matrix_ref, mat, local.at[5])
    fetch.start()
    own_panel = pltpu.make_async_copy(panel_ref, pall.at[z], local.at[0])
    own_panel.start()
    barrier = pltpu.get_barrier_semaphore()

    def hello(device):
        pl.semaphore_signal(barrier, inc=1, device_id=device, device_id_type=MESH)

    for d in range(1, NZ):
        hello(dev(z=lax.rem(z + d, NZ)))
    for d in range(1, NX):
        hello(dev(x=lax.rem(x + d, NX)))
    for d in range(1, NY):
        hello(dev(y=lax.rem(y + d, NY)))
    hello(partner)
    near = NZ + NX + NY - 2

    @pl.when(is_root)
    def _():
        @pl.loop(1, 2 * CHIPS)
        def _(q):
            hello((q, z))

    @pl.when(jnp.logical_not(is_root))
    def _():
        hello((0, z))

    p_r = prow_ref[...]
    c_r = chip_of(p_r)
    here = c_r == chip
    before = (iota((NB, NB), 0) < iota((NB, NB), 1)).astype(BF16)
    rank = mm(jnp.broadcast_to(here.astype(BF16), (16, NB)), before)[:1].astype(I32)
    mine_at = here & (rank == iota((CAP, NB), 0))
    row = jnp.sum(jnp.where(mine_at, (p_r + 1).astype(F32), 0.0), axis=1, keepdims=True).astype(I32) - 1
    pick = (row - pr * rows) == iota((CAP, rows), 1)
    sel[...] = (pick & (row >= NB)).astype(F32)
    keep_sel = pltpu.make_async_copy(sel, sel_ref, local.at[6])
    fetch.wait()
    got = select_rows(pick.astype(BF16), mat[...])
    contrib[0] = got[:, :half]
    contrib[1] = got[:, half:]
    own_panel.wait()

    @pl.when(is_root & (z < NB // 64))
    def _():
        at = iota((64, NB), 1) == iota((64, NB), 0) + 64 * z
        pan = panel_ref[...]
        hi, mid, low = split3(pan)
        onto = at.astype(BF16)
        to = ((1,), (1,))
        diag = (mm(low, onto, to) + mm(mid, onto, to)) + mm(hi, onto, to)
        inv = halves_inverse(diag, 64)
        hi, mid, low = split3(inv)
        back = (mm(low, onto) + mm(mid, onto)) + mm(hi, onto)
        col = iota((64, NB), 1)
        low_src[...] = jnp.where((col >= 64 * z) & (col < 64 * z + 64), back, pan)

    @pl.when(is_root)
    def _():
        pl.semaphore_wait(barrier, near + 2 * CHIPS - 1)

    @pl.when(jnp.logical_not(is_root))
    def _():
        pl.semaphore_wait(barrier, near + 1)

    def line(mine):
        other = 1 - mine
        n1, n2 = (NX, NY) if mine == 0 else (NY, NX)
        a1, a2 = (x, y) if mine == 0 else (y, x)
        peer1 = (lambda i: dev(x=i)) if mine == 0 else (lambda i: dev(y=i))
        peer2 = (lambda i: dev(y=i)) if mine == 0 else (lambda i: dev(x=i))
        slots = slots_all.at[mine]
        lows = low_all.at[mine]
        low_root = is_root & (z < NB // 64)
        has_low = (z < NB // 64) & (lax.rem(z, 2) == mine)
        top_here = is_root if mine == 0 else (pr < 0)

        def part(ref):
            if mine == 0:
                return lambda b, h: ref.at[b, pl.ds(2 * h, 2)]
            return lambda b, h: ref.at[pl.ds(4 * h, 4), b]

        zr = Ring(NZ, z, lambda b, h: pall.at[b, pl.ds(32 * h, 32)],
                  lambda i: dev(z=i), z_send, z_recv)
        ring = Ring(n2, a2, part(slots), peer2, r_send, r_recv)
        lring = Ring(n2, a2, part(lows), peer2, q_send, q_recv)
        last = n2 // 2 - 1
        pair = lambda: remote(contrib.at[other], from_pair, pair_send, pair_recv, partner)
        keep = lambda: pltpu.make_async_copy(own, slots.at[y, x], local.at[2])
        keep_low = lambda: pltpu.make_async_copy(low_in, lows.at[y, x, z // 2], local.at[3])

        def spread(d):
            return remote(own, slots.at[y, x], one_send.at[d], one_recv.at[d],
                          peer1(lax.rem(a1 + d, n1)))

        def lspread(d):
            return remote(lows.at[y, x], lows.at[y, x], lone_send.at[d], lone_recv.at[d],
                          peer1(lax.rem(a1 + d, n1)))

        def zspread(d):
            return remote(low_in, lows.at[y, x, z // 2], zl_send.at[d], zl_recv.at[z // 2],
                          dev(z=lax.rem(z + d, NZ)))

        def spread_wait(ref, ss, rs):
            for d in range(1, n1):
                src = lax.rem(a1 + n1 - d, n1)
                dst = ref.at[y, src] if mine == 0 else ref.at[src, x]
                remote(dst, dst, ss.at[d], rs.at[d], peer1(src)).wait_recv()

        def to_pair(block, h):
            ref = part(slots)(block, h)
            remote(ref, ref, slot_send, slot_recv, partner).start()

        def seg0():
            zr.step(0)

            @pl.when(low_root)
            def _():
                @pl.loop(0, CHIPS)
                def _(q):
                    src = low_src.at[pl.ds(pl.multiple_of(q // NX * 8, 8), 8),
                                       pl.ds(pl.multiple_of(lax.rem(q, NX) * 128, 128), 128)]

                    @pl.when((q > 0) | (lax.rem(z, 2) == 1))
                    def _():
                        remote(src, low_in, sc_send.at[q], sc_recv,
                               (q * 2 + lax.rem(z, 2), z)).start()

            pair().start()

            @pl.when(is_root & has_low)
            def _():
                tile = pltpu.make_async_copy(low_src.at[pl.ds(0, 8), pl.ds(0, 128)], low_in, local.at[1])
                tile.start()
                tile.wait()

            pair().wait_recv()
            own[...] = contrib[mine] + from_pair[...]
            keep().start()
            for d in range(1, n1):
                spread(d).start()

        def seg1():
            @pl.when(has_low)
            def _():
                @pl.when(jnp.logical_not(top_here))
                def _():
                    remote(low_in, low_in, sc_send.at[0], sc_recv, partner).wait_recv()
                keep_low().start()
                for d in range(1, NZ):
                    zspread(d).start()
            zr.step(1)

        def seg2():
            zr.step(2)
            for i in range(4):
                @pl.when(z != 2 * i + mine)
                def _():
                    ref = lows.at[y, x, i]
                    remote(ref, ref, zl_send.at[1], zl_recv.at[i], partner).wait_recv()

            @pl.when(has_low)
            def _():
                keep_low().wait()
            for d in range(1, n1):
                lspread(d).start()
            keep().wait()
            spread_wait(slots, one_send, one_recv)
            ring.step(0)
            for h in (0, 1):
                to_pair(a2, h)

        def seg3():
            zr.step(3)
            spread_wait(lows, lone_send, lone_recv)
            lring.step(0)
            ring.step(1, to_pair)

        def seg4():
            zr.step(4)
            lring.step(1)
            if last >= 2:
                ring.step(2, to_pair)

        def seg5():
            zr.step(5)
            if last >= 3:
                lring.step(2)
                ring.step(3, to_pair)
                lring.step(3)
            ring.finish(to_pair)
            if mine == 0:
                @pl.when(is_root)
                def _():
                    remote(staged.at[0, 0, 1], tops.at[1], top_send.at[0, 1], top_recv, partner).start()
                    for c in (0, 1):
                        for q in (1, 3):
                            via(q, c).start()

                    @pl.loop(1, CHIPS)
                    def _(q):
                        xx, yy = lax.rem(q, NX), q // NX

                        @pl.when((lax.rem(xx, 2) == 0) | (yy == 0))
                        def _():
                            for c in (0, 1):
                                remote(staged.at[yy, xx, c], tops.at[c], top_send.at[q, c], top_recv,
                                       (q * 2 + c, z)).start()
            lring.finish()
            remote(lows, lows, lpair_send, lpair_recv, partner).start()
            ref = slots_all.at[other]
            remote(ref, ref, slot_send, slot_recv, partner).wait_recv()

        def via(q, c):
            return remote(staged.at[pl.ds(1, NY - 1), q, c], relay,
                          rl_send.at[q // 2, c], rl_recv, (q * 2 + c, z))

        def seg6():
            ref = low_all.at[other]
            remote(ref, ref, lpair_send, lpair_recv, partner).wait_recv()

        relays = (y == 0) & (lax.rem(x, 2) == 1)

        def onward(i):
            return remote(relay.at[i], tops.at[mine], rs_send.at[i], top_recv, dev(y=i + 1))

        def seg7():
            zr.finish()

            @pl.when(relays)
            def _():
                remote(relay, relay, rl_send.at[0, 0], rl_recv, partner).wait_recv()
                for i in range(NY - 1):
                    onward(i).start()

        def tpair():
            return remote(tops.at[mine], tops.at[mine], tp_send, tp_recv, partner)

        def seg8():
            @pl.when(jnp.logical_not(top_here))
            def _():
                remote(tops.at[mine], tops.at[mine], top_send.at[0, 0], top_recv, partner).wait_recv()
            if mine == 0:
                @pl.when(is_root)
                def _():
                    first = pltpu.make_async_copy(staged.at[0, 0, 0], tops.at[0], local.at[4])
                    first.start()
                    first.wait()
            tpair().start()
            ref = tops.at[other]
            remote(ref, ref, tp_send, tp_recv, partner).wait_recv()

        def seg9():
            pair().wait_send()
            for d in range(1, n1):
                spread(d).wait_send()
                lspread(d).wait_send()
            remote(lows, lows, lpair_send, lpair_recv, partner).wait_send()
            tpair().wait_send()
            ring.drain()
            lring.drain()
            zr.drain()
            remote(slots, slots, slot_send, slot_recv, partner).wait_send()

            @pl.when(has_low)
            def _():
                for d in range(1, NZ):
                    zspread(d).wait_send()

            @pl.when(low_root & (mine == 0))
            def _():
                @pl.loop(0, CHIPS)
                def _(q):
                    @pl.when((q > 0) | (lax.rem(z, 2) == 1))
                    def _():
                        remote(low_in, low_in, sc_send.at[q], sc_recv, partner).wait_send()

            @pl.when(relays)
            def _():
                for i in range(NY - 1):
                    onward(i).wait_send()

            if mine == 0:
                @pl.when(is_root)
                def _():
                    remote(staged.at[0, 0, 1], tops.at[1], top_send.at[0, 1], top_recv, partner).wait_send()
                    for c in (0, 1):
                        for q in (1, 3):
                            via(q, c).wait_send()

                    @pl.loop(1, CHIPS)
                    def _(q):
                        xx, yy = lax.rem(q, NX), q // NX

                        @pl.when((lax.rem(xx, 2) == 0) | (yy == 0))
                        def _():
                            for c in (0, 1):
                                remote(staged.at[yy, xx, c], tops.at[c], top_send.at[q, c], top_recv,
                                       partner).wait_send()

        return [seg0, seg1, seg2, seg3, seg4, seg5, seg6, seg7, seg8, seg9]

    segments = [line(0), line(1)]

    def run(k):
        for mine in (0, 1):
            pl.when(core == mine)(segments[mine][k])

    def column(v):
        wide = jnp.broadcast_to(v.astype(F32), (128, NB)).T.astype(I32)
        return jnp.concatenate([wide] * (NB // 128), axis=1)

    def top_index():
        p_c = column(p_r)
        c_c = chip_of(p_c)
        i0, i1 = iota((NB, NB), 0), iota((NB, NB), 1)
        d_r = c_r * CAP + count((c_c == c_r) & (i0 < i1), 0)
        t_r = iota((1, NB), 1)
        left_rank = t_r - count(p_c < t_r, 0)
        chosen = count(p_c == t_r, 0) > 0
        vac_rank = count((p_c >= NB) & (p_c < p_r), 0)
        keys[0:1] = d_r
        keys[1:2] = jnp.where(chosen, -2, left_rank)
        keys[2:3] = jnp.where(p_r >= NB, vac_rank + 1, 0)
        for i, piece in enumerate(split3(mat[:NB])):
            parts[i] = piece

    def top_piece(g):
        n = 8 * CAP
        e = keys[0:1] == g * n + iota((n, NB), 0)
        key = jnp.sum(jnp.where(e, keys[2:3].astype(F32), 0.0), axis=1, keepdims=True).astype(I32) - 1
        onehot = (key == keys[1:2]).astype(BF16)
        res = (mm(onehot, parts[2]) + mm(onehot, parts[1])) + mm(onehot, parts[0])
        for c in (0, 1):
            staged[pl.ds(2 * g, 2), :, c] = res[:, c * half:c * half + half].reshape(2, NX, CAP, half)

    def on_root(*work):
        @pl.when(is_root)
        def _():
            for w in work:
                w()

    run(0)
    keep_sel.start()
    on_root(top_index, lambda: top_piece(0))
    run(1)
    run(2)
    on_root(lambda: top_piece(1), lambda: top_piece(2))
    p_c = column(p_r)
    c_c = chip_of(p_c)
    slot_c = jnp.sum(((c_c == c_r) & (iota((NB, NB), 1) < iota((NB, NB), 0))).astype(F32),
                     axis=1, keepdims=True)
    most_ref[0] = jnp.max(slot_c)
    dest = c_c[:, :128] * CAP + jnp.broadcast_to(slot_c.astype(I32), (NB, 128))
    for k in range(CHIPS * CAP // 128):
        perm[:, 128 * k:128 * k + 128] = (dest == iota((NB, 128), 1) + 128 * k).astype(BF16)
    run(3)
    on_root(lambda: top_piece(3))
    run(4)
    run(5)
    for n in (0, 1):
        upper[:, n * half:n * half + half] = select_rows(
            perm[...], slots_all[n].reshape(CHIPS * CAP, half))
    run(6)
    for i in range(NB // 64):
        for yy in range(NY):
            for xx in range(NX):
                if 128 * xx < 64 * i + 64:
                    lower[64 * i + 8 * yy:64 * i + 8 * yy + 8, 128 * xx:128 * xx + 128] = (
                        low_all[i % 2, yy, xx, i // 2])
    i0, i1 = iota((128, 128), 0), iota((128, 128), 1)
    for k in range(4):
        block = lower[128 * k:128 * k + 128, 128 * k:128 * k + 128]
        two = jnp.where((i0 // 64) == (i1 // 64), block, 0.0)
        off = jnp.where(i0 // 64 > i1 // 64, block, 0.0)
        inverse[k] = two - hdot(two, hdot(off, two))
    run(7)
    keep_panel = pltpu.make_async_copy(pall, p_ref, local.at[7])
    keep_panel.start()

    def keep_upper(i):
        return pltpu.make_async_copy(upper.at[pl.ds(128 * i, 128)], u_ref.at[pl.ds(128 * i, 128)],
                                     local.at[8 + i])

    for i in range(4):
        rhs = upper[128 * i:128 * i + 128]
        if i:
            rhs = rhs - hdot(lower[128 * i:128 * i + 128, :128 * i], upper[:128 * i])
        upper[128 * i:128 * i + 128] = hdot(inverse[i], rhs)
        keep_upper(i).start()
    run(8)
    keep_tops = pltpu.make_async_copy(tops, tops_ref, local.at[12])
    keep_tops.start()
    run(9)
    keep_tops.wait()
    keep_sel.wait()
    keep_panel.wait()
    for i in range(4):
        keep_upper(i).wait()


def step(p_row, panel, matrix):
    rows, cols = matrix.shape
    half = cols // 2
    dma = pltpu.SemaphoreType.DMA
    vm = pl.BlockSpec(memory_space=pltpu.VMEM)
    anyspec = pl.BlockSpec(memory_space=pl.ANY)
    v = pltpu.VMEM
    return pl.pallas_call(
        step_kernel,
        out_shape=(
            jax.ShapeDtypeStruct((NB, cols), F32),
            jax.ShapeDtypeStruct((NZ,) + panel.shape, F32),
            jax.ShapeDtypeStruct((2, CAP, half), F32),
            jax.ShapeDtypeStruct((CAP, rows), F32),
            jax.ShapeDtypeStruct((1,), F32),
        ),
        in_specs=[vm, vm, anyspec],
        out_specs=(anyspec,) * 4 + (pl.BlockSpec(memory_space=pltpu.SMEM),),
        scratch_shapes=[
            v((rows, cols), F32), v((NZ,) + panel.shape, F32),
            v((2, NY, NX, CAP, half), F32), v((2, NY, NX, 4, 8, 128), F32),
            v((2, CAP, half), F32), v((NY, NX, 2, CAP, half), F32), v((NY - 1, CAP, half), F32),
            v((CAP, half), F32), v((2, CAP, half), F32), v((CAP, half), F32), v((8, 128), F32),
            v((8, NB), I32), v((3, NB, cols), BF16),
            v((64, NB), F32), v((NB, NB), F32), v((4, 128, 128), F32), v((NB, CHIPS * CAP), BF16),
            v((NB, cols), F32), v((CAP, rows), F32),
            dma((2, NZ // 2, 2)), dma((2, NZ // 2, 2)),
            dma((2, NY // 2, 2)), dma((2, NY // 2, 2)),
            dma((2, NY // 2, 2)), dma((2, NY // 2, 2)),
            dma((NY,)), dma((NY,)), dma((NY,)), dma((NY,)),
            dma((NZ,)), dma((4,)), dma((CHIPS,)), dma, dma((13,)),
            dma, dma, dma, dma, dma, dma, dma((CHIPS, 2)), dma, dma, dma,
            dma((2, 2)), dma, dma((NY - 1,)),
        ],
        compiler_params=pltpu.CompilerParams(collective_id=0, has_side_effects=True),
        name="step",
    )(p_row, panel, matrix)


def update_kernel(me_ref, m_ref, p_ref, u_ref, tops_ref, sel_ref, out_ref, u_hi, u_lo):
    i = pl.program_id(0)
    half = tops_ref.shape[2]
    block = out_ref.shape[0]

    @pl.when(i == 0)
    def _():
        u = u_ref[...]
        hi = u.astype(BF16)
        u_hi[...] = hi
        u_lo[...] = (u - hi.astype(F32)).astype(BF16)

    p = p_ref[...]
    p_hi = p.astype(BF16)
    p_lo = (p - p_hi.astype(F32)).astype(BF16)
    product = (mm(p_lo, u_hi[...]) + mm(p_hi, u_lo[...])) + mm(p_hi, u_hi[...])
    sel = sel_ref[...].astype(BF16)
    replaced = mm(sel, jnp.ones((CAP, 128), BF16), ((0,), (0,)))[:, :1] > 0.5
    incoming = jnp.concatenate([select_rows(sel, tops_ref[n], ((0,), (0,))) for n in (0, 1)], axis=1)
    out_ref[...] = jnp.where(replaced, incoming, m_ref[...]) - product

    @pl.when((me_ref[0] == 0) & (i < NB // block))
    def _():
        out_ref[...] = u_ref[pl.ds(i * block, block)]


def update(me, matrix, pall, upper, tops, sel):
    rows, cols = matrix.shape
    block = 256
    whole = lambda shape: pl.BlockSpec(shape, lambda n: (0,) * len(shape))
    return pl.pallas_call(
        update_kernel,
        grid=(rows // block,),
        out_shape=jax.ShapeDtypeStruct(matrix.shape, F32),
        in_specs=[
            pl.BlockSpec(memory_space=pltpu.SMEM),
            pl.BlockSpec((block, cols), lambda n: (n, 0)),
            pl.BlockSpec((block, NB), lambda n: (n, 0)),
            whole(upper.shape), whole(tops.shape),
            pl.BlockSpec((CAP, block), lambda n: (0, n)),
        ],
        out_specs=pl.BlockSpec((block, cols), lambda n: (n, 0)),
        scratch_shapes=[pltpu.VMEM((NB, cols), BF16), pltpu.VMEM((NB, cols), BF16)],
        name="update",
    )(me, matrix, pall.reshape(rows, NB), upper, tops, sel)


def ring_sum(value, axis):
    n = lax.axis_size(axis)
    pairs = [(i, (i + 1) % n) for i in range(n)]

    def body(_, carry):
        total, moving = carry
        moving = lax.ppermute(moving, axis, pairs)
        return total + moving, moving

    return lax.fori_loop(0, n - 1, body, (value, value))[0]


def dense(matrix, panel, pivot_rows):
    own_rows = matrix.shape[0]
    row = lax.axis_index("prow")
    col = lax.axis_index("pcol")
    row_base = row * own_rows
    slab = jnp.zeros((lax.axis_size("pcol"),) + panel.shape, F32)
    panels = ring_sum(lax.dynamic_update_slice(slab, panel[None], (col, 0, 0)), "pcol")
    panels = panels.reshape(own_rows, NB)
    local_rows = pivot_rows - row_base
    owned = (local_rows >= 0) & (local_rows < own_rows)
    picked = (local_rows[:, None] == jnp.arange(own_rows, dtype=I32)[None, :]).astype(F32)
    picked = jnp.dot(picked, matrix, precision=HIGHEST, preferred_element_type=F32)
    first = jnp.where(row == 0, 1.0, 0.0)
    pack = jnp.concatenate([picked, matrix[:NB] * first], axis=1)
    pack = jnp.concatenate([pack, panels[:NB] * first], axis=1)
    pack = ring_sum(pack, "prow")
    own_cols = matrix.shape[1]
    new_top, top_rows, lower = pack[:, :own_cols], pack[:, own_cols:2 * own_cols], pack[:, 2 * own_cols:]

    def solve_row(j, upper):
        coef = lax.dynamic_slice(lower, (j, 0), (1, NB))
        coef = jnp.where(jnp.arange(NB)[None, :] < j, coef, 0.0)
        done = jnp.dot(coef, upper, precision=HIGHEST, preferred_element_type=F32)
        mine = lax.dynamic_slice(upper, (j, 0), (1, own_cols)) - done
        return lax.dynamic_update_slice(upper, mine, (j, 0))

    upper = lax.fori_loop(0, NB, solve_row, new_top)
    vacated = pivot_rows >= NB
    top_index = jnp.arange(NB, dtype=I32)
    chosen = jnp.any(pivot_rows[None, :] == top_index[:, None], axis=1)
    left_rank = top_index - jnp.sum((pivot_rows[None, :] < top_index[:, None]).astype(I32), axis=1)
    vac_rank = jnp.sum((vacated[None, :] & (pivot_rows[None, :] < pivot_rows[:, None])).astype(I32), axis=1)
    pairing = (vacated[:, None] & jnp.logical_not(chosen)[None, :]
               & (left_rank[None, :] == vac_rank[:, None])).astype(F32)
    incoming = jnp.dot(pairing, top_rows, precision=HIGHEST, preferred_element_type=F32)
    global_rows = row_base + jnp.arange(own_rows, dtype=I32)
    place = (global_rows[:, None] == pivot_rows[None, :]) & vacated[None, :]
    moved = jnp.dot(place.astype(F32), incoming, precision=HIGHEST, preferred_element_type=F32)
    swapped = jnp.where(jnp.any(place, axis=1)[:, None], moved, matrix)
    updated = swapped - jnp.dot(panels, upper, precision=HIGHEST, preferred_element_type=F32)
    top_fill = jnp.pad(upper, ((0, own_rows - NB), (0, 0)))
    return jnp.where((global_rows < NB)[:, None], top_fill, updated)


def shards(matrix, panel, pivot_rows):
    me = lax.axis_index("prow").reshape(1)
    upper, pall, tops, sel, most = step(pivot_rows.reshape(1, NB), panel, matrix)
    return lax.cond(most[0] < CAP,
                    lambda: update(me, matrix, pall, upper, tops, sel),
                    lambda: dense(matrix, panel, pivot_rows))


def solution(mesh):
    return jax.shard_map(
        shards,
        mesh=mesh,
        in_specs=(P("prow", "pcol"), P(("prow", "pcol"), None), P()),
        out_specs=P("prow", "pcol"),
        check_vma=False,
    )
```
